256 devices in a mesh: sector: 64 (over x_lo, y, z), radial: 2 (over x_hi), col: 2 (over core).
Axes of the slice: x: 4 (x_hi: 2, x_lo: 2; x = x_hi * 2 + x_lo), y: 4, z: 8, core: 2. Of those that a mesh axis runs over, the one named last changes fastest.
Arguments:
- correction_guess: float32 [8, 3, 256, 32, 128], P('col', None, 'sector', 'radial'), may hold values from -24 to 24
- ritz_residual: float32 [8, 3, 256, 32, 128], P('col', None, 'sector', 'radial'), may hold values from -36 to 36
- ritz_basis: float32 [8, 3, 256, 32, 128], P('col', None, 'sector', 'radial'), may hold values from -8 to 8
- diagonal: float32 [256, 32, 128], P('sector', 'radial'), may hold values from 0.25 to 2
- coupling: float32 [3, 3], replicated, may hold values from -0.3 to 2, as said below
- class_ids: int32 [64], P('sector'), may hold values from 0 to 7
- class_stiffness: float32 [8], replicated, may hold values from 0.7 to 1.4
- shifts: float32 [8], P('col'), may hold values from 0.1 to 0.5
- contact_dest: int32 [32768, 1], P(('sector', 'radial')), may hold values from 0 to 63; in each aligned block of 256 rows (0 to 255, 256 to 511, ...) at most 8 rows name the same one
- contact_source: int32 [32768], P(('sector', 'radial')), may hold values from 0 to 8191
- contact_target: int32 [32768], P(('sector', 'radial')), may hold values from 0 to 8191
- contact_stiffness: float32 [32768], P(('sector', 'radial')), may hold values from 0.5 to 2
Outputs:
- correction: float32 [8, 3, 256, 32, 128], P('col', None, 'sector', 'radial')
- inner_residual: float32 [8, 3, 256, 32, 128], P('col', None, 'sector', 'radial')
The draws below stay inside these ranges and needn't reach their ends.
Inputs may be any that keep to these rules, and one draw needn't show every extreme that they name: `contact_dest`: in the rows of one device no sector is named more than 8 times, and one sector exactly 8 times. `coupling`: diagonal entries between 1 and 2.
All inputs are finite; a program needn't handle non-finite values.
Results may differ from the reference program's by a relative error of at most 0.0002.
Values sent between devices are 32-bit elements; how exact they have to be, the bound alone decides.
A program may use at most 64 MiB of HBM per device.

```python
import math
import jax
import jax.numpy as jnp
import numpy as np
from jax import lax

CHANNELS = 3
COLS = 8
TANG = 4
RLOC = 16
AX = 128
CROWS = 256
ITERS = 3
NCLASS = 8
SECTORS = 64
TANGTOT = 256
RADIAL = 32
CAP = 8
CONTACTS = 32768
DOFS = 3145728
N_RADIAL = 2


def basis_draw(key):
    shape = (COLS, CHANNELS, TANGTOT, RADIAL, AX)
    sector_index = (lax.broadcasted_iota(jnp.int32, shape, 2) // TANG).astype(jnp.float32)
    ramp = 0.6 * jnp.exp(math.log(3.0) * sector_index / max(SECTORS - 1, 1))
    raw_values = jnp.clip(jax.random.normal(jax.random.fold_in(key, 11), shape, jnp.float32), -4.0, 4.0)
    return raw_values * ramp


def mixed_draw(key, first_salt, second_salt, weight):
    shape = (COLS, CHANNELS, TANGTOT, RADIAL, AX)
    noise_part = jnp.clip(jax.random.normal(jax.random.fold_in(key, first_salt), shape, jnp.float32), -4.0, 4.0)
    amounts = jax.random.uniform(jax.random.fold_in(key, second_salt), (COLS, COLS), jnp.float32, -weight, weight)
    base_vectors = basis_draw(key)
    columns = []
    for target_column in range(COLS):
        running = noise_part[target_column]
        for source_column in range(COLS):
            running = running + amounts[source_column, target_column] * base_vectors[source_column]
        columns.append(running)
    return jnp.stack(columns)


def draw_ritz_basis(key, part):
    return basis_draw(key)


def draw_ritz_residual(key, part):
    return mixed_draw(key, 12, 13, 0.5)


def draw_correction_guess(key, part):
    return mixed_draw(key, 14, 15, 0.3)


def draw_coupling(key, part):
    diag_part = jax.random.uniform(jax.random.fold_in(key, 21), (CHANNELS, CHANNELS), jnp.float32, 1.0, 2.0)
    off_part = jax.random.uniform(jax.random.fold_in(key, 22), (CHANNELS, CHANNELS), jnp.float32, -0.3, 0.3)
    return jnp.where(jnp.eye(CHANNELS, dtype=jnp.float32) > 0.5, diag_part, off_part)


def place_ends(values, rng, least, top_value):
    longest = values.shape.index(max(values.shape))
    spots = []
    for shift in (0, 1):
        where = [jax.random.randint(jax.random.fold_in(rng, axis), (), 0, length) for axis, length in enumerate(values.shape)]
        where[longest] = (where[longest] + shift) % values.shape[longest]
        spots.append(tuple(where))
    return values.at[spots[0]].set(least).at[spots[1]].set(top_value)


def block_scale(stream_key, shape, split, low, high):
    gain, own = 1.0, jax.random.fold_in(stream_key, 6)
    for position, shards_of in split:
        steps = jnp.exp(jax.random.uniform(jax.random.fold_in(own, position), (shards_of,), jnp.float32, low / len(split), high / len(split)))
        gain = gain * jnp.repeat(steps, shape[position] // shards_of).reshape([-1 if axis == position else 1 for axis in range(len(shape))])
    return gain


def shared_out(key, own, number, rows, number_of, top, most, lean):
    order = jax.random.permutation(key, number_of)
    packed, common = shares(number_of, rows * top, most, lean, True), shares(number_of, rows * top, most, lean, False)
    places = jnp.arange(number_of)

    def named(tallies, turn):
        used = int((tallies > 0).sum())
        fixed = max(1, used // 4)
        moved = fixed + (places - fixed + turn * (used - fixed)) % max(1, number_of - fixed)
        return jnp.zeros((number_of,), jnp.int32).at[order[jnp.where(places < fixed, places, moved)]].set(jnp.asarray(tallies, jnp.int32))

    tallies = jnp.where(number % 4 == 0, named(packed, number // 4), named(common, number - number // 4 - 1))
    mixed = jax.random.permutation(jax.random.fold_in(own, 3), number_of)
    source_of, sink = mixed[0:number_of // 2 * 2:2], mixed[1:number_of // 2 * 2:2]
    slack = jnp.minimum(tallies[source_of] - 1, most - tallies[sink]) // 2
    slack = jnp.where((source_of == order[0]) | (sink == order[0]) | (tallies[sink] == 0), 0, jnp.maximum(slack, 0))
    moved = jax.random.randint(jax.random.fold_in(own, 4), (number_of // 2,), 0, 1 << 20) % (slack + 1)
    tallies = tallies.at[source_of].add(-moved).at[sink].add(moved)
    labels = jnp.searchsorted(jnp.cumsum(tallies), jnp.arange(rows * top), side="right").astype(jnp.int32)
    listing = labels.reshape(top, rows).T
    listing = listing[jax.random.permutation(jax.random.fold_in(own, 1), rows)]
    turn = jax.random.randint(jax.random.fold_in(own, 2), (rows, 1), 0, top)
    return jnp.take_along_axis(listing, (jnp.arange(top)[None, :] + turn) % top, axis=1)


def shares(number_of, total, most, skew, full):
    portions = [(1 << 20) // math.isqrt(standing ** skew) + 1 for standing in range(1, number_of + 1)]
    largest = most if full else min(most, max(-(-total // number_of), total * portions[0] // sum(portions)))
    least = 1 if total - largest >= number_of - 1 else 0
    counts, spare = [largest] + [least] * (number_of - 1), total - largest - least * (number_of - 1)
    while spare > 0:
        free = [i for i in range(1, number_of) if counts[i] < largest] or [i for i in range(1, number_of) if counts[i] < most]
        pool, remaining = sum([portions[i] for i in free]), spare
        for i in free:
            more = min(most - counts[i], max(1, remaining * portions[i] // pool), spare)
            counts[i] = counts[i] + more
            spare = spare - more
    return np.array(counts)


def setup_inputs(seed: int = 0) -> dict:
    key_of = jax.random.split(jax.random.key(seed), 13)
    correction_guess = draw_correction_guess(jax.random.fold_in(key_of[12], 71), 0)
    ritz_residual = draw_ritz_residual(jax.random.fold_in(key_of[12], 71), 0)
    ritz_basis = draw_ritz_basis(jax.random.fold_in(key_of[12], 71), 0)
    diagonal = jnp.clip(jnp.exp(math.log(2.0) - 2.0794415 * jax.random.uniform(key_of[3], (TANGTOT, RADIAL, AX), jnp.float32) ** block_scale(key_of[3], (TANGTOT, RADIAL, AX), ((0, 64), (1, 2)), -0.2, 0.2)), 0.25, 2.0)
    coupling = draw_coupling(jax.random.fold_in(key_of[12], 71), 0)
    class_ids = place_ends(jax.random.randint(key_of[5], (SECTORS,), 0, NCLASS), jax.random.fold_in(key_of[5], 1), 0, NCLASS - 1).astype(jnp.int32)
    class_stiffness = jnp.clip(jnp.exp(jax.random.uniform(key_of[6], (NCLASS,), jnp.float32, math.log(0.7), math.log(1.4))), 0.7, 1.4)
    shifts = jnp.clip(0.1 + 0.4 * jax.random.uniform(key_of[7], (COLS,), jnp.float32) ** block_scale(key_of[7], (COLS,), ((0, 2),), -0.2, 0.2), 0.1, 0.5)
    contact_dest_keys = jax.random.split(jax.random.fold_in(key_of[8], 1), CONTACTS // CROWS)
    contact_dest_turns = jax.random.permutation(jax.random.fold_in(key_of[8], 3), CONTACTS // CROWS)
    contact_dest = jax.vmap(lambda own, number: shared_out(jax.random.fold_in(key_of[8], 2), own, number, CROWS, SECTORS, 1, CAP, 2))(contact_dest_keys, contact_dest_turns).reshape((CONTACTS, 1))
    contact_source = place_ends(jax.random.randint(key_of[9], (CONTACTS,), 0, TANG * RLOC * AX), jax.random.fold_in(key_of[9], 1), 0, (TANG * RLOC * AX) - 1).astype(jnp.int32)
    contact_target = place_ends(jax.random.randint(key_of[10], (CONTACTS,), 0, TANG * RLOC * AX), jax.random.fold_in(key_of[10], 1), 0, (TANG * RLOC * AX) - 1).astype(jnp.int32)
    contact_stiffness = jnp.clip(jnp.exp(math.log(2.0) - 1.3862944 * jax.random.uniform(key_of[11], (CONTACTS,), jnp.float32) ** block_scale(key_of[11], (CONTACTS,), ((0, 128),), -0.2, 0.2)), 0.5, 2.0)
    return {"correction_guess": correction_guess, "ritz_residual": ritz_residual, "ritz_basis": ritz_basis, "diagonal": diagonal, "coupling": coupling, "class_ids": class_ids, "class_stiffness": class_stiffness, "shifts": shifts, "contact_dest": contact_dest, "contact_source": contact_source, "contact_target": contact_target, "contact_stiffness": contact_stiffness}


def cell_laplace(blocks):
    tangent = jnp.roll(blocks, 1, 2) + jnp.roll(blocks, -1, 2)
    padded = jnp.pad(blocks, ((0, 0), (0, 0), (0, 0), (1, 1), (1, 1)))
    radial_pair = padded[:, :, :, 2:, 1:-1] + padded[:, :, :, :-2, 1:-1]
    axial_pair = padded[:, :, :, 1:-1, 2:] + padded[:, :, :, 1:-1, :-2]
    return 6.0 * blocks - tangent - radial_pair - axial_pair


def global_cell(sector_index, slab_index, cell_number):
    tang_index = cell_number // (RLOC * AX)
    slab_row = (cell_number // AX) % RLOC
    axial_index = cell_number % AX
    row_index = slab_index * RLOC + slab_row
    return ((sector_index * TANG + tang_index) * RADIAL + row_index) * AX + axial_index


def reference(correction_guess, ritz_residual, ritz_basis, diagonal, coupling, class_ids, class_stiffness, shifts, contact_dest, contact_source, contact_target, contact_stiffness):
    sector_stiff = class_stiffness[class_ids]
    stiff_cells = jnp.repeat(sector_stiff, TANG)[None, None, :, None, None]
    off_diag = coupling * (1.0 - jnp.eye(CHANNELS, dtype=jnp.float32))
    on_diag = jnp.diagonal(coupling)[None, :, None, None, None]
    shift_field = shifts[:, None, None, None, None]
    jacobi = stiff_cells * 6.0 * on_diag + diagonal[None, None] - shift_field
    row_block = jnp.arange(CONTACTS, dtype=jnp.int32) // CROWS
    sector_of = row_block // N_RADIAL
    slab_of = row_block % N_RADIAL
    source_index = global_cell(sector_of, slab_of, contact_source)
    target_index = global_cell(contact_dest[:, 0], slab_of, contact_target)

    def apply_shifted(blocks):
        laplace_term = cell_laplace(blocks)
        mixed_term = jnp.einsum("cd,jdtrz->jctrz", off_diag, blocks, precision=lax.Precision.HIGHEST) + on_diag * laplace_term
        applied = stiff_cells * mixed_term + diagonal[None, None] * blocks - shift_field * blocks
        flattened = blocks.reshape(COLS * CHANNELS, -1)
        forces = flattened[:, source_index] * contact_stiffness[None, :]
        updated = applied.reshape(COLS * CHANNELS, -1).at[:, target_index].add(forces)
        return updated.reshape(blocks.shape)

    def project(blocks):
        coefficients = jnp.einsum("ictrz,jctrz->ij", ritz_basis, blocks, precision=lax.Precision.HIGHEST) / DOFS
        return blocks - jnp.einsum("ij,ictrz->jctrz", coefficients, ritz_basis, precision=lax.Precision.HIGHEST)

    correction = correction_guess
    inner_residual = correction_guess
    for sweep in range(ITERS):
        applied = apply_shifted(project(correction))
        inner_residual = -ritz_residual - project(applied)
        correction = correction + 0.7 * project(inner_residual / jacobi)
    return correction, inner_residual
```

```python
import functools

import jax
import jax.numpy as jnp
from jax import lax
from jax.experimental import pallas as pl
from jax.experimental.pallas import tpu as pltpu
from jax.sharding import Mesh
from jax.sharding import PartitionSpec as P

SECTOR = ("sector_0", "sector_1", "sector_2")
SECTOR_RADIAL = ("sector_0", "sector_1", "sector_2", "radial")
DAMPING = 0.7
NX, NY, NZ = 2, 4, 8
NP = NX * NY
F32 = jnp.float32
BF16 = jnp.bfloat16
MESH_ID = pl.DeviceIdType.MESH
NT = (((1,), (1,)), ((), ()))


def split2(x):
    hi = x.astype(BF16)
    return hi, (x - hi.astype(F32)).astype(BF16)


def iota(shape, dim):
    return lax.broadcasted_iota(jnp.int32, shape, dim).astype(F32)


def kernel(
    dofs,
    dst_r, src_r, tgt_r, kst_r, kap, cid, cst, shf, c0_h, rho_h, q_h, dg_h,
    oc_h, or_h,
    u, rho, q, dg, ij, w, d,
    ut, qt, dgt, dgs, ijt, dt,
    us, qs, ijs, ds,
    ur, qr, ijr, dr, rsnd,
    lsm, rsm, ltm, rtm, wbuf,
    cs1a, cr1a, cs2a, cr2a, cs1, cr1, cs2, cr2,
    rm, rs1, rr1, rs2, rr2,
    cf, st_s, mt_s, acf,
    ld_sem, out_sem, snd, rcv,
):
    x = lax.axis_index("sector_0")
    y = lax.axis_index("sector_1")
    z = lax.axis_index("sector_2")
    ri = lax.axis_index("radial")
    me_col = lax.axis_index("col")
    p = x * NY + y
    pq = ri * NP + p

    def zpeer(k):
        return {"sector_2": (z + k) % NZ}

    def plane(k):
        o = (pq + k) % (2 * NP)
        return {"radial": o // NP, "sector_0": (o // NY) % NX, "sector_1": o % NY}

    def ppeer(k):
        o = (p + k) % NP
        return {"sector_0": o // NY, "sector_1": o % NY}

    c1 = (z + 1) // NZ
    c2 = (y + c1) // NY
    nxt = {"sector_2": (z + 1) % NZ, "sector_1": (y + c1) % NY, "sector_0": (x + c2) % NX}
    b1 = 1 - (z + NZ - 1) // NZ
    b2 = 1 - (y + NY - b1) // NY
    prv = {"sector_2": (z + NZ - 1) % NZ, "sector_1": (y + NY - b1) % NY, "sector_0": (x + NX - b2) % NX}
    across = {"radial": 1 - ri}
    twin = {"col": 1 - me_col}

    barrier = pltpu.get_barrier_semaphore()

    def sig(dev):
        pl.semaphore_signal(barrier, inc=1, device_id=dev, device_id_type=MESH_ID)

    for k in range(1, NZ):
        sig(zpeer(k))
    for k in range(1, 2 * NP):
        sig(plane(k))
    sig(nxt)
    sig(prv)
    sig(twin)

    loads = [
        pltpu.make_async_copy(q_h, q.at[pl.ds(0, 4)], ld_sem.at[0]),
        pltpu.make_async_copy(c0_h, u, ld_sem.at[1]),
        pltpu.make_async_copy(dg_h, dg, ld_sem.at[2]),
        pltpu.make_async_copy(rho_h, rho, ld_sem.at[3]),
    ]
    for c in loads:
        c.start()

    count = [0]
    pending = []

    def rcopy(src, dst, dev, idx):
        return pltpu.make_async_remote_copy(
            src_ref=src, dst_ref=dst, send_sem=snd.at[idx], recv_sem=rcv.at[idx],
            device_id=dev, device_id_type=MESH_ID,
        )

    def send(src, dst, dev):
        idx = count[0]
        count[0] += 1
        c = rcopy(src, dst, dev, idx)
        c.start()
        pending.append(c)
        return c

    def group(n, peer, src_of, dst):
        idx = count[0]
        count[0] += 1

        def one(k, carry):
            rcopy(src_of(k), dst, peer(k), idx).start()
            return carry

        lax.fori_loop(1, n, one, 0)
        return idx

    def await_group(buf, n, idx):
        part = buf.at[pl.ds(0, n)]
        pltpu.make_async_copy(part, part, rcv.at[idx]).wait()

    def drain_group(buf, n, idx):
        part = buf.at[pl.ds(0, n)]
        pltpu.make_async_copy(part, part, snd.at[idx]).wait()

    stiff = cst[cid[0]]

    meta = [r[...].astype(F32) for r in (dst_r, src_r, tgt_r, kst_r)]

    def flat_row(m):
        return jnp.concatenate([m[0:1, :], m[1:2, :]], axis=1)

    dest = flat_row(meta[0])
    later = iota((128, 256), 1)
    rank = jnp.zeros((1, 256), F32)
    for h in range(2):
        column = jnp.broadcast_to(meta[0][h : h + 1, :], (128, 128)).T
        column = jnp.concatenate([column, column], axis=1)
        hit = (column == dest) & (iota((128, 256), 0) + 128.0 * h < later)
        rank = rank + jnp.sum(jnp.where(hit, 1.0, 0.0), axis=0, keepdims=True)
    dp = jnp.floor(dest * 0.125)
    slot = rank * 64.0 + (dest - 8.0 * dp) * 8.0 + dp
    source, target, kst = flat_row(meta[1]), flat_row(meta[2]), flat_row(meta[3])
    s_row = jnp.floor(source * (1.0 / 128.0))
    t_row = jnp.floor(target * (1.0 / 128.0))
    k_hi = kst.astype(BF16).astype(F32)
    k_mid = (kst - k_hi).astype(BF16).astype(F32)
    k_lo = kst - k_hi - k_mid
    rows = jnp.concatenate(
        [s_row, source - 128.0 * s_row, t_row, target - 128.0 * t_row, k_hi, k_mid, k_lo, jnp.ones((1, 256), F32)],
        axis=0,
    ).astype(BF16)
    onehot = jnp.where(iota((512, 256), 0) == slot, 1.0, 0.0).astype(BF16)
    packed = lax.dot_general(rows, onehot, NT, preferred_element_type=F32)
    valid = packed[7:8, :] > 0.5
    src_row = jnp.where(valid, packed[0:1, :], -1.0)
    picks = jnp.where(iota((128, 512), 0) == packed[1:2, :], 1.0, 0.0).astype(BF16)
    lsm[...] = jnp.concatenate([picks, picks], axis=0)
    rsm[...] = jnp.where(iota((64, 512), 0) == src_row, 1.0, 0.0)
    tgt = packed[2:3, :] * 128.0 + packed[3:4, :]
    kpk = packed[4:5, :] + packed[5:6, :] + packed[6:7, :]

    pl.semaphore_wait(barrier, (NZ - 1) + (2 * NP - 1) + 3)

    def edge_rows(ref, j, c):
        top = ref[j, c, pl.ds(15, 4, stride=16), :]
        bottom = ref[j, c, pl.ds(0, 4, stride=16), :]
        return jnp.where(ri == 0, top, bottom)

    def pack_radial(ref, out, spare):
        for j in range(4):
            tail = spare if (spare is not None and j == 0) else jnp.zeros((4, 128), F32)
            out[j] = jnp.concatenate([edge_rows(ref, j, c) for c in range(3)] + [tail], axis=0)

    def send_tangent(ref, dst):
        a = send(ref.at[:, :, pl.ds(48, 16), :], dst.at[0], nxt)
        b = send(ref.at[:, :, pl.ds(0, 16), :], dst.at[1], prv)
        return a, b

    def gather(ref, base):
        def column(j, carry):
            xs = jnp.concatenate([ref[j, c] for c in range(3)], axis=0)
            both = jnp.concatenate(split2(xs), axis=1)
            got = jnp.dot(both, lsm[...], preferred_element_type=F32)
            for c in range(3):
                picked = jnp.sum(got[c * 64 : (c + 1) * 64] * rsm[...], axis=0, keepdims=True)
                for sh in range(4):
                    wbuf[base + j * 4 + c, pl.ds(sh, 1), :] = picked[:, sh * 128 : (sh + 1) * 128]
            return carry

        for j in range(4):
            column(j, 0)

    def spare_rows(base, j, row):
        for sh in range(4):
            wbuf[base + j * 4 + 3, pl.ds(sh, 1), :] = row[:, sh * 128 : (sh + 1) * 128]

    def message(base):
        m = wbuf[pl.ds(base, 16)].reshape(64, 128)
        turned = jnp.concatenate([m, m], axis=0).T
        lane = lax.broadcasted_iota(jnp.int32, (64, 128), 1)
        return jnp.where(lane < 64, turned[0:64], turned[64:128])

    def unpack(m):
        both = jnp.concatenate([m, pltpu.roll(m, 64, 1)], axis=0).T
        return both[0:64].reshape(4, 16, 128)

    def fold_dots(ref, vref):
        def block(b, acc):
            c, r = b // 8, pl.multiple_of((b % 8) * 8, 8)
            qv = [q[i, c, pl.ds(r, 8), :] for i in range(8)]
            out = []
            for j in range(4):
                v = vref[j, c, pl.ds(r, 8), :]
                for i in range(8):
                    out.append(acc[j * 8 + i] + qv[i] * v)
            return tuple(out)

        acc = lax.fori_loop(0, 24, block, tuple(jnp.zeros((8, 128), F32) for _ in range(32)))
        for k in range(32):
            ref[pl.ds(k, 1), :] = jnp.sum(acc[k], axis=0, keepdims=True)

    def gram(ref, scale):
        pairs = [(a, b) for a in range(8) for b in range(a, 8)]

        def block(b, acc):
            c, r = b // 8, pl.multiple_of((b % 8) * 8, 8)
            qv = [q[i, c, pl.ds(r, 8), :] for i in range(8)]
            sv = qv if scale is None else [t * ij[scale, c, pl.ds(r, 8), :] for t in qv]
            return tuple(acc[n] + sv[a] * qv[e] for n, (a, e) in enumerate(pairs))

        acc = lax.fori_loop(0, 24, block, tuple(jnp.zeros((8, 128), F32) for _ in pairs))
        for n, (a, e) in enumerate(pairs):
            row = jnp.sum(acc[n], axis=0, keepdims=True)
            ref[pl.ds(a * 8 + e, 1), :] = row
            if a != e:
                ref[pl.ds(e * 8 + a, 1), :] = row

    def lane_totals(block):
        return jnp.sum(block.T, axis=0, keepdims=True)

    def spread(row):
        return jnp.broadcast_to(row * (1.0 / dofs), (128, 128)).T

    def reduce_start(rnd, nr):
        idx = group(
            NZ, zpeer, lambda k: rs1.at[rnd, pl.ds(0, nr)], rr1.at[rnd, z, pl.ds(0, nr)]
        )
        rr1[rnd, z, pl.ds(0, nr)] = rs1[rnd, pl.ds(0, nr)]
        return idx

    def reduce_middle(rnd, nr, idx):
        part = rr1.at[rnd, pl.ds(0, NZ - 1), pl.ds(0, nr)]
        pltpu.make_async_copy(part, part, rcv.at[idx]).wait()
        total = rr1[rnd, 0, pl.ds(0, nr)]
        for k in range(1, NZ):
            total = total + rr1[rnd, k, pl.ds(0, nr)]
        rs2[rnd, pl.ds(0, nr)] = total
        idx2 = group(
            2 * NP, plane, lambda k: rs2.at[rnd, pl.ds(0, nr)], rr2.at[rnd, pq, pl.ds(0, nr)]
        )
        rr2[rnd, pq, pl.ds(0, nr)] = total
        return idx2

    def reduce_end(rnd, nr, idx):
        part = rr2.at[rnd, pl.ds(0, 2 * NP - 1), pl.ds(0, nr)]
        pltpu.make_async_copy(part, part, rcv.at[idx]).wait()
        total = rr2[rnd, 0, pl.ds(0, nr)]
        for k in range(1, 2 * NP):
            total = total + rr2[rnd, k, pl.ds(0, nr)]
        return total

    def reduce_drain(rnd, nr, idx1, idx2):
        part = rr1.at[rnd, pl.ds(0, NZ - 1), pl.ds(0, nr)]
        pltpu.make_async_copy(part, part, snd.at[idx1]).wait()
        part = rr2.at[rnd, pl.ds(0, 2 * NP - 1), pl.ds(0, nr)]
        pltpu.make_async_copy(part, part, snd.at[idx2]).wait()

    def exchange_start(s1, r1):
        idx = group(NZ, zpeer, lambda k: s1.at[(z + k) % NZ], r1.at[z])
        r1[z] = s1[z]
        return idx

    def exchange_middle(r1, s2, r2, idx, g):
        await_group(r1, NZ - 1, idx)
        for k in range(NP):
            for e in range(g):
                s2[k, pl.ds(e * 8, 8), :] = r1[:, e * 8 + k, :]
        idx2 = group(NP, ppeer, lambda k: s2.at[(p + k) % NP], r2.at[p])
        r2[p] = s2[p]
        return idx2

    loads[0].wait()
    swap_q = send(q.at[pl.ds(0, 4)], q.at[pl.ds(4, 4)], twin)
    halo_q = send_tangent(q.at[pl.ds(0, 4)], qt.at[:, pl.ds(0, 4)])
    loads[1].wait()
    halo_c = send_tangent(u, ut)
    loads[2].wait()
    splat = jnp.full((8, 128), stiff, F32)
    dgs[0] = jnp.concatenate([dg[48:64, :], splat], axis=0)
    dgs[1] = jnp.concatenate([dg[0:16, :], splat], axis=0)
    halo_d = (send(dgs.at[0], dgt.at[0], nxt), send(dgs.at[1], dgt.at[1], prv))
    dg_edge = jnp.where(ri == 0, dg[pl.ds(15, 4, stride=16), :], dg[pl.ds(0, 4, stride=16), :])
    pack_radial(u, rsnd.at[0], dg_edge)
    pack_radial(q, rsnd.at[1], None)
    side_c = send(rsnd.at[0], ur, across)
    side_q = send(rsnd.at[1], qr.at[pl.ds(0, 4)], across)

    gather(u, 0)
    gather(q, 16)
    got = jnp.dot(jnp.concatenate(split2(dg[...]), axis=1), lsm[...], preferred_element_type=F32)
    spare_rows(0, 0, jnp.sum(got * rsm[...], axis=0, keepdims=True))
    spare_rows(0, 1, tgt)
    spare_rows(0, 2, jnp.full((1, 512), stiff, F32))
    spare_rows(0, 3, kpk)
    for j in range(4):
        spare_rows(16, j, jnp.zeros((1, 512), F32))
    for e in range(2):
        cs1a[:, pl.ds(e * 8, 8), :] = message(16 * e).reshape(NZ, 8, 128)
    xa1 = exchange_start(cs1a, cr1a)

    for j in range(4):
        for c in range(3):
            ij[j, c] = 1.0 / (stiff * 6.0 * kap[c, c] + dg[...] - shf[j])

    swap_q.wait_recv()
    rm[pl.ds(96, 32), :] = jnp.zeros((32, 128), F32)
    fold_dots(rm, u)
    gram(rm.at[pl.ds(32, 64)], None)
    rs1[0, 0] = lane_totals(rm[pl.ds(0, 128), :])
    ra1 = reduce_start(0, 1)

    for j in range(4):
        gram(rm.at[pl.ds(128 + j * 64, 64)], j)

    ra2 = reduce_middle(0, 1, ra1)
    xa2 = exchange_middle(cr1a, cs2a, cr2a, xa1, 2)

    for e in range(2):
        rs1[1, 1 + e] = lane_totals(rm[pl.ds(128 + e * 128, 128), :])

    for c in halo_d + halo_q + halo_c + (side_c, side_q):
        c.wait_recv()
    swap_t = send(qt.at[:, pl.ds(0, 4)], qt.at[:, pl.ds(4, 4)], twin)
    swap_r = send(qr.at[pl.ds(0, 4)], qr.at[pl.ds(4, 4)], twin)
    for side in range(2):
        sv = jnp.concatenate([dgt[side, 16:24, :], dgt[side, 16:24, :]], axis=0)
        dv = dgt[side, 0:16, :]
        for j in range(4):
            for c in range(3):
                ijt[side, j, c] = 1.0 / (sv * 6.0 * kap[c, c] + dv - shf[j])
    dv = ur[0, 12:16, :]
    base = jnp.concatenate([stiff * 6.0 * kap[c, c] + dv for c in range(3)] + [jnp.full((4, 128), 2.0, F32)], axis=0)
    for j in range(4):
        ijr[j] = 1.0 / (base - shf[j])

    await_group(cr2a, NP - 1, xa2)
    us[...] = unpack(cr2a[:, pl.ds(0, 8), :].reshape(64, 128))
    qs[pl.ds(0, 4)] = unpack(cr2a[:, pl.ds(8, 8), :].reshape(64, 128))
    swap_s = send(qs.at[pl.ds(0, 4)], qs.at[pl.ds(4, 4)], twin)
    dv = us[0, 12:16, :]
    sv = us[2, 12:16, :]
    base = jnp.concatenate([sv * 6.0 * kap[c, c] + dv for c in range(3)] + [jnp.full((4, 128), 2.0, F32)], axis=0)
    for j in range(4):
        ijs[j] = 1.0 / (base - shf[j])
    kr = us[3, 12:16, :]
    for sh in range(4):
        tv = us[1, 12 + sh : 13 + sh, :]
        tr = jnp.floor(tv * (1.0 / 128.0))
        tl = tv - 128.0 * tr
        lanes = slice(sh * 128, (sh + 1) * 128)
        rtm[:, lanes] = jnp.where(iota((64, 128), 0) == tr, 1.0, 0.0) * kr[sh : sh + 1, :]
        lands = jnp.where(iota((128, 128), 0) == tl, 1.0, 0.0).astype(BF16)
        ltm[:, lanes] = lands
        ltm[:, 512 + sh * 128 : 640 + sh * 128] = lands

    total = reduce_end(0, 1, ra2)
    wide = spread(total[0])
    acf[...] = wide[0:32].reshape(4, 8, 128)
    st_s[...] = wide[32:96].reshape(8, 8, 128)

    def mix(coef, j, qv):
        n = qv[0].shape[0]
        acc = None
        for i in range(8):
            term = jnp.broadcast_to(coef[j, pl.ds(i, 1), :], (n, 128)) * qv[i]
            acc = term if acc is None else acc + term
        return acc

    regions = (
        (12, lambda b: (b // 4, pl.multiple_of((b % 4) * 16, 16)),
         lambda r, j, a: r[j, a[0], pl.ds(a[1], 16), :], (u, q, ij, d)),
        (6, lambda b: (b // 3, b % 3),
         lambda r, j, a: r[a[0], j, a[1]], (ut, qt, ijt, dt)),
        (1, lambda b: b, lambda r, j, a: r[j], (us, qs, ijs, ds)),
        (1, lambda b: b, lambda r, j, a: r[j], (ur, qr, ijr, dr)),
    )

    def put(region, j, a, v):
        if region == 0:
            u[j, a[0], pl.ds(a[1], 16), :] = v
        elif region == 1:
            ut[a[0], j, a[1]] = v
        elif region == 2:
            us[j] = v
        else:
            ur[j] = v

    def first_update(which):
        for n in which:
            blocks, place, get, (ru, rq, _, _) = regions[n]

            def step(b, carry):
                a = place(b)
                qv = [get(rq, i, a) for i in range(8)]
                for j in range(4):
                    put(n, j, a, get(ru, j, a) - mix(acf, j, qv))
                return carry

            lax.fori_loop(0, blocks, step, 0)

    def update(rnd):
        for n in range(4):
            blocks, place, get, (ru, rq, rj, rd) = regions[n]

            def step(b, carry):
                a = place(b)
                qv = [get(rq, i, a) for i in range(8)]
                for j in range(4):
                    new = get(ru, j, a) + DAMPING * get(rd.at[rnd], j, a)
                    new = new + get(rj, j, a) * mix(cf.at[0], j, qv) - mix(cf.at[1], j, qv)
                    put(n, j, a, new)
                return carry

            lax.fori_loop(0, blocks, step, 0)

    for c in halo_c:
        c.wait_send()
        pending[:] = [t for t in pending if t is not c]
    first_update((0,))
    swap_t.wait_recv()
    swap_r.wait_recv()
    swap_s.wait_recv()
    first_update((1, 2, 3))

    row_in = lax.broadcasted_iota(jnp.int32, (64, 128), 0) % 16
    lane_in = lax.broadcasted_iota(jnp.int32, (64, 128), 1)
    edge = row_in == 15 * (1 - ri)

    def apply(dref):
        def column(j, carry):
            hs = []
            for c in range(3):
                hrow, lrow = [], []
                for sh in range(4):
                    v = us[j, pl.ds(c * 4 + sh, 1), :]
                    a = rtm[:, sh * 128 : (sh + 1) * 128] * v
                    ah, al = split2(a)
                    hrow.append(ah)
                    lrow.append(al)
                hs.append(jnp.concatenate(hrow + lrow, axis=1))
            touch = lax.dot_general(jnp.concatenate(hs, axis=0), ltm[...], NT, preferred_element_type=F32)
            xs = [u[j, c] for c in range(3)]
            for c in range(3):
                v = xs[c]
                before = jnp.concatenate([ut[0, j, c], v[0:48]], axis=0)
                after = jnp.concatenate([v[16:64], ut[1, j, c]], axis=0)
                lap = 6.0 * v - before - after
                lap = lap - jnp.where(row_in == 0, 0.0, pltpu.roll(v, 1, 0))
                lap = lap - jnp.where(row_in == 15, 0.0, pltpu.roll(v, 63, 0))
                beside = jnp.concatenate(
                    [jnp.broadcast_to(ur[j, pl.ds(c * 4 + t, 1), :], (16, 128)) for t in range(4)], axis=0
                )
                lap = lap - jnp.where(edge, beside, 0.0)
                lap = lap - jnp.where(lane_in == 0, 0.0, pltpu.roll(v, 1, 1))
                lap = lap - jnp.where(lane_in == 127, 0.0, pltpu.roll(v, 127, 1))
                mixed = kap[c, c] * lap
                for e in range(3):
                    if e != c:
                        mixed = mixed + kap[c, e] * xs[e]
                out = stiff * mixed + (dg[...] - shf[j]) * v + touch[c * 64 : (c + 1) * 64]
                w[j, c] = out
                dref[j, c] = -(rho[j, c] + out) * ij[j, c]
            return carry

        lax.fori_loop(0, 4, column, 0)

    def coefficients(row, final):
        wide = spread(row)
        for j in range(4):
            b = wide[j * 8 : j * 8 + 8]
            e = wide[32 + j * 8 : 40 + j * 8]
            for i in range(8):
                e = e + mt_s[j, i] * b[i : i + 1, :]
            a = acf[j]
            if final:
                cf[0, j] = b
                cf[1, j] = a - DAMPING * e
            else:
                se = st_s[0] * e[0:1, :]
                for i in range(1, 8):
                    se = se + st_s[i] * e[i : i + 1, :]
                cf[0, j] = DAMPING * b
                cf[1, j] = DAMPING * (2.0 * e - se)
                acf[j] = a + DAMPING * (e - se)

    loads[3].wait()
    drains = []
    for rnd in range(3):
        last = rnd == 2
        nr = 3 if rnd == 0 else 1
        dref = d.at[rnd]
        apply(dref)
        if not last:
            pack_radial(dref, rsnd.at[2 + rnd], None)
            halo = send_tangent(dref, dt.at[rnd])
            side = send(rsnd.at[2 + rnd], dr.at[rnd], across)
            gather(dref, 0)
            cs1[rnd] = message(0).reshape(NZ, 8, 128)
            x1 = exchange_start(cs1.at[rnd], cr1.at[rnd])
        fold_dots(rm, w)
        fold_dots(rm.at[pl.ds(32, 32)], dref)
        rs1[rnd + 1, 0] = lane_totals(rm[pl.ds(0, 128), :])
        r1 = reduce_start(rnd + 1, nr)
        if not last:
            x2 = None
        r2 = reduce_middle(rnd + 1, nr, r1)
        drains.append((rnd + 1, nr, r1, r2))
        if not last:
            x2 = exchange_middle(cr1.at[rnd], cs2.at[rnd], cr2.at[rnd], x1, 1)
            for c in halo + (side,):
                c.wait_recv()
        total = reduce_end(rnd + 1, nr, r2)
        if rnd == 0:
            for e in range(2):
                mt_s[pl.ds(2 * e, 2)] = spread(total[1 + e]).reshape(2, 8, 8, 128)
        coefficients(total[0], last)
        if not last:
            await_group(cr2.at[rnd], NP - 1, x2)
            ds[rnd] = unpack(cr2[rnd].reshape(64, 128))
            update(rnd)
            drains.append((rnd, x1, x2))

    def finish(b, carry):
        c, r = b // 4, pl.multiple_of((b % 4) * 16, 16)
        here = (c, pl.ds(r, 16))
        qv = [q[i, c, pl.ds(r, 16), :] for i in range(8)]
        for j in range(4):
            res = mix(cf.at[0], j, qv) - rho[j, c, pl.ds(r, 16), :] - w[j, c, pl.ds(r, 16), :]
            new = u[j, c, pl.ds(r, 16), :] + DAMPING * res * ij[j, c, pl.ds(r, 16), :] + mix(cf.at[1], j, qv)
            w[j, c, pl.ds(r, 16), :] = res
            rho[j, c, pl.ds(r, 16), :] = new
        return carry

    lax.fori_loop(0, 12, finish, 0)
    outs = [
        pltpu.make_async_copy(rho, oc_h, out_sem.at[0]),
        pltpu.make_async_copy(w, or_h, out_sem.at[1]),
    ]
    for c in outs:
        c.start()
    for c in pending:
        c.wait_send()
    drain_group(cr1a, NZ - 1, xa1)
    drain_group(cr2a, NP - 1, xa2)
    reduce_drain(0, 1, ra1, ra2)
    for t in drains:
        if len(t) == 4:
            reduce_drain(*t)
        else:
            drain_group(cr1.at[t[0]], NZ - 1, t[1])
            drain_group(cr2.at[t[0]], NP - 1, t[2])
    for c in outs:
        c.wait()


def body(
    correction_guess, ritz_residual, ritz_basis, diagonal, coupling, class_ids,
    class_stiffness, shifts, contact_dest, contact_source, contact_target, contact_stiffness,
):
    cols, chans, tang, rloc, ax = correction_guess.shape
    devices = NX * NY * NZ * 2
    dofs = float(chans * tang * rloc * ax * devices)
    flat = (cols, chans, tang * rloc, ax)
    vm = pltpu.VMEM
    own = (4, 3, 64, 128)
    sheet = (4, 3, 16, 128)
    small = (4, 16, 128)
    scratch = [
        vm(own, F32), vm(own, F32), vm((8, 3, 64, 128), F32), vm((64, 128), F32), vm(own, F32), vm(own, F32),
        vm((3,) + own, F32),
        vm((2,) + sheet, F32), vm((2, 8, 3, 16, 128), F32), vm((2, 24, 128), F32), vm((2, 24, 128), F32),
        vm((2,) + sheet, F32), vm((2, 2) + sheet, F32),
        vm(small, F32), vm((8, 16, 128), F32), vm(small, F32), vm((2,) + small, F32),
        vm(small, F32), vm((8, 16, 128), F32), vm(small, F32), vm((2,) + small, F32), vm((4,) + small, F32),
        vm((256, 512), BF16), vm((64, 512), F32), vm((128, 1024), BF16), vm((64, 512), F32), vm((32, 4, 128), F32),
        vm((NZ, 16, 128), F32), vm((NZ, 16, 128), F32), vm((NP, 16, 128), F32), vm((NP, 16, 128), F32),
        vm((2, NZ, 8, 128), F32), vm((2, NZ, 8, 128), F32), vm((2, NP, 8, 128), F32), vm((2, NP, 8, 128), F32),
        vm((384, 128), F32), vm((4, 3, 1, 128), F32), vm((4, NZ, 3, 1, 128), F32), vm((4, 3, 1, 128), F32),
        vm((4, 2 * NP, 3, 1, 128), F32),
        vm((2, 4, 8, 128), F32), vm((8, 8, 128), F32), vm((4, 8, 8, 128), F32), vm((4, 8, 128), F32),
        pltpu.SemaphoreType.DMA((4,)), pltpu.SemaphoreType.DMA((2,)),
        pltpu.SemaphoreType.DMA((36,)), pltpu.SemaphoreType.DMA((36,)),
    ]
    anyspace = pl.BlockSpec(memory_space=pl.ANY)
    smem = pl.BlockSpec(memory_space=pltpu.SMEM)
    correction, residual = pl.pallas_call(
        functools.partial(kernel, dofs),
        out_shape=(jax.ShapeDtypeStruct(flat, F32), jax.ShapeDtypeStruct(flat, F32)),
        in_specs=[pl.BlockSpec(memory_space=pltpu.VMEM)] * 4 + [smem] * 4 + [pl.BlockSpec(memory_space=pltpu.HBM)] * 4,
        out_specs=(anyspace, anyspace),
        scratch_shapes=scratch,
        compiler_params=pltpu.CompilerParams(collective_id=0, has_side_effects=True, vmem_limit_bytes=16 * 1024 * 1024),
        name="sweeps",
    )(
        contact_dest.reshape(2, 128), contact_source.reshape(2, 128), contact_target.reshape(2, 128),
        contact_stiffness.reshape(2, 128), coupling, class_ids, class_stiffness, shifts,
        *(pltpu.with_memory_space_constraint(a, pltpu.HBM) for a in (
            correction_guess.reshape(flat), ritz_residual.reshape(flat), ritz_basis.reshape(flat),
            diagonal.reshape(tang * rloc, ax),
        )),
    )
    shape = correction_guess.shape
    return correction.reshape(shape), residual.reshape(shape)


def solution(mesh):
    split = Mesh(
        mesh.devices.reshape(NX, NY, NZ, mesh.shape["radial"], mesh.shape["col"]),
        ("sector_0", "sector_1", "sector_2", "radial", "col"),
    )
    field = P("col", None, SECTOR, "radial", None)
    placed = (
        field, field, field, P(SECTOR, "radial", None), P(), P(SECTOR), P(), P("col"),
        P(SECTOR_RADIAL, None), P(SECTOR_RADIAL), P(SECTOR_RADIAL), P(SECTOR_RADIAL),
    )
    return jax.shard_map(body, mesh=split, in_specs=placed, out_specs=(field, field), check_vma=False)
```

```python
import functools

import jax
import jax.numpy as jnp
from jax import lax
from jax.experimental import pallas as pl
from jax.experimental.pallas import tpu as pltpu
from jax.sharding import Mesh
from jax.sharding import PartitionSpec as P

SECTOR = ("sector_0", "sector_1", "sector_2")
SECTOR_RADIAL = ("sector_0", "sector_1", "sector_2", "radial")
DAMPING = 0.7
NX, NY, NZ = 2, 4, 8
NS = NX * NY * NZ
SIZES = {"sector_0": NX, "sector_1": NY, "sector_2": NZ, "radial": 2}


def peer_offsets():
    along_x = {(0, 0): 0, (1, 0): 1, (0, 1): 2, (1, 1): 1}
    found = []
    for dr in range(2):
        for dx in range(NX):
            for dy in range(NY):
                for dz in range(NZ):
                    hops = along_x[dx, dr] + min(dy, NY - dy) + min(dz, NZ - dz)
                    steps = (("sector_0", dx), ("sector_1", dy), ("sector_2", dz), ("radial", dr))
                    if hops:
                        found.append((-hops, tuple(t for t in steps if t[1])))
    return [t[1] for t in sorted(found, key=lambda t: t[0])]


OFFSETS = peer_offsets()
F32 = jnp.float32
BF16 = jnp.bfloat16
MESH_ID = pl.DeviceIdType.MESH
NT = (((1,), (1,)), ((), ()))


def split2(x):
    hi = x.astype(BF16)
    return hi, (x - hi.astype(F32)).astype(BF16)


def iota(shape, dim):
    return lax.broadcasted_iota(jnp.int32, shape, dim).astype(F32)


def kernel(
    dofs,
    dst_r, src_r, tgt_r, kst_r, kap, cid, cst, shf, c0_h, rho_h, q_h, dg_h,
    oc_h, or_h,
    u, rho, q, dg, ij, w, d,
    ut, qt, dgt, dgs, ijt, dt,
    us, qs, ijs, ds,
    ur, qr, ijr, dr, rsnd,
    lsm, rsm, ltm, rtm, wbuf, amat, land, krow,
    pa, ra, pb, rb, pc, rc, pd, rd,
    rm,
    cf, st_s, mt_s, acf,
    ld_sem, out_sem, snd, rcv,
):
    x = lax.axis_index("sector_0")
    y = lax.axis_index("sector_1")
    z = lax.axis_index("sector_2")
    ri = lax.axis_index("radial")
    me_col = lax.axis_index("col")

    here = {"sector_0": x, "sector_1": y, "sector_2": z, "radial": ri}

    def peer(offset):
        place = {}
        for name, step in offset:
            at = here[name] + step
            place[name] = jnp.where(at >= SIZES[name], at - SIZES[name], at)
        return place

    def sector_of(place):
        return (place.get("sector_0", x) * NY + place.get("sector_1", y)) * NZ + place.get("sector_2", z)

    me = sector_of({})
    me_row = ri * NS + me

    c1 = (z + 1) // NZ
    c2 = (y + c1) // NY
    nxt = {"sector_2": (z + 1) % NZ, "sector_1": (y + c1) % NY, "sector_0": (x + c2) % NX}
    b1 = 1 - (z + NZ - 1) // NZ
    b2 = 1 - (y + NY - b1) // NY
    prv = {"sector_2": (z + NZ - 1) % NZ, "sector_1": (y + NY - b1) % NY, "sector_0": (x + NX - b2) % NX}
    across = {"radial": 1 - ri}
    twin = {"col": 1 - me_col}

    barrier = pltpu.get_barrier_semaphore()

    def sig(dev):
        pl.semaphore_signal(barrier, inc=1, device_id=dev, device_id_type=MESH_ID)

    for offset in OFFSETS:
        sig(peer(offset))
    sig(twin)

    loads = [
        pltpu.make_async_copy(q_h, q.at[pl.ds(0, 4)], ld_sem.at[0]),
        pltpu.make_async_copy(c0_h, u, ld_sem.at[1]),
        pltpu.make_async_copy(dg_h, dg, ld_sem.at[2]),
        pltpu.make_async_copy(rho_h, rho, ld_sem.at[3]),
    ]
    for c in loads:
        c.start()

    count = [0]
    pending = []

    def rcopy(src, dst, dev, idx):
        return pltpu.make_async_remote_copy(
            src_ref=src, dst_ref=dst, send_sem=snd.at[idx], recv_sem=rcv.at[idx],
            device_id=dev, device_id_type=MESH_ID,
        )

    def send(src, dst, dev):
        idx = count[0]
        count[0] += 1
        c = rcopy(src, dst, dev, idx)
        c.start()
        pending.append(c)
        return c

    def exchange(planes, rbuf, same, other):
        (a0, an), (b0, bn) = same, other
        idx = count[0]
        count[0] += 2
        for offset in OFFSETS:
            place = peer(offset)
            across_slab = "radial" in place
            first, num = (b0, bn) if across_slab else (a0, an)
            if num == 0:
                continue
            row = sector_of(place)
            rcopy(
                planes.at[pl.ds(first, num), pl.ds(row, 1)],
                rbuf.at[pl.ds(first, num), pl.ds(me_row, 1)],
                place, idx + int(across_slab),
            ).start()
        for e in range(a0, a0 + an):
            rbuf[e, pl.ds(me_row, 1), :] = planes[e, pl.ds(me, 1), :]

        def finish(sem):
            if an:
                part = rbuf.at[pl.ds(a0, an), pl.ds(0, NS - 1)]
                pltpu.make_async_copy(part, part, sem.at[idx]).wait()
            if bn:
                part = rbuf.at[pl.ds(b0, bn), pl.ds(0, NS)]
                pltpu.make_async_copy(part, part, sem.at[idx + 1]).wait()

        drains.append(lambda: finish(snd))
        return lambda: finish(rcv)

    drains = []

    stiff = cst[cid[0]]

    meta = [r[...].astype(F32) for r in (dst_r, src_r, tgt_r, kst_r)]

    def flat_row(m):
        return jnp.concatenate([m[0:1, :], m[1:2, :]], axis=1)

    dest = flat_row(meta[0])
    later = iota((128, 256), 1)
    rank = jnp.zeros((1, 256), F32)
    for h in range(2):
        column = jnp.broadcast_to(meta[0][h : h + 1, :], (128, 128)).T
        column = jnp.concatenate([column, column], axis=1)
        hit = (column == dest) & (iota((128, 256), 0) + 128.0 * h < later)
        rank = rank + jnp.sum(jnp.where(hit, 1.0, 0.0), axis=0, keepdims=True)
    slot = rank * 64.0 + dest
    source, target, kst = flat_row(meta[1]), flat_row(meta[2]), flat_row(meta[3])
    s_row = jnp.floor(source * (1.0 / 128.0))
    t_row = jnp.floor(target * (1.0 / 128.0))
    k_hi = kst.astype(BF16).astype(F32)
    k_mid = (kst - k_hi).astype(BF16).astype(F32)
    k_lo = kst - k_hi - k_mid
    rows = jnp.concatenate(
        [s_row, source - 128.0 * s_row, t_row, target - 128.0 * t_row, k_hi, k_mid, k_lo, jnp.ones((1, 256), F32)],
        axis=0,
    ).astype(BF16)
    onehot = jnp.where(iota((512, 256), 0) == slot, 1.0, 0.0).astype(BF16)
    packed = lax.dot_general(rows, onehot, NT, preferred_element_type=F32)
    valid = packed[7:8, :] > 0.5
    src_row = jnp.where(valid, packed[0:1, :], -1.0)
    picks = jnp.where(iota((128, 512), 0) == packed[1:2, :], 1.0, 0.0).astype(BF16)
    lsm[...] = jnp.concatenate([picks, picks], axis=0)
    rsm[...] = jnp.where(iota((64, 512), 0) == src_row, 1.0, 0.0)
    tgt = packed[2:3, :] * 128.0 + packed[3:4, :]
    kpk = packed[4:5, :] + packed[5:6, :] + packed[6:7, :]

    def edge_rows(ref, j, c):
        top = ref[j, c, pl.ds(15, 4, stride=16), :]
        bottom = ref[j, c, pl.ds(0, 4, stride=16), :]
        return jnp.where(ri == 0, top, bottom)

    def pack_radial(ref, out, spare):
        for j in range(4):
            tail = spare if (spare is not None and j == 0) else jnp.zeros((4, 128), F32)
            out[j] = jnp.concatenate([edge_rows(ref, j, c) for c in range(3)] + [tail], axis=0)

    def send_tangent(ref, dst):
        a = send(ref.at[:, :, pl.ds(48, 16), :], dst.at[0], nxt)
        b = send(ref.at[:, :, pl.ds(0, 16), :], dst.at[1], prv)
        return a, b

    def gather(ref, base):
        def column(j, carry):
            xs = jnp.concatenate([ref[j, c] for c in range(3)], axis=0)
            both = jnp.concatenate(split2(xs), axis=1)
            got = jnp.dot(both, lsm[...], preferred_element_type=F32)
            for c in range(3):
                picked = jnp.sum(got[c * 64 : (c + 1) * 64] * rsm[...], axis=0, keepdims=True)
                for sh in range(4):
                    wbuf[base + j * 4 + c, pl.ds(sh, 1), :] = picked[:, sh * 128 : (sh + 1) * 128]
            return carry

        for j in range(4):
            column(j, 0)

    def spare_rows(base, j, row):
        for sh in range(4):
            wbuf[base + j * 4 + 3, pl.ds(sh, 1), :] = row[:, sh * 128 : (sh + 1) * 128]

    def message(base):
        m = wbuf[pl.ds(base, 16)].reshape(64, 128)
        turned = jnp.concatenate([m, m], axis=0).T
        lane = lax.broadcasted_iota(jnp.int32, (64, 128), 1)
        return jnp.where(lane < 64, turned[0:64], turned[64:128])

    def unpack(m):
        both = jnp.concatenate([m, pltpu.roll(m, 64, 1)], axis=0).T
        return both[0:64].reshape(4, 16, 128)

    def fold_dots(ref, vref, half):
        lead = half * 4

        def block(b, acc):
            c, r = b // 4, pl.multiple_of((b % 4) * 16, 16)
            out = list(acc)
            for e in range(2):
                qv = [q[lead + i, c, pl.ds(r + 8 * e, 8), :] for i in range(4)]
                vv = [vref[j, c, pl.ds(r + 8 * e, 8), :] for j in range(4)]
                for j in range(4):
                    for i in range(4):
                        out[j * 4 + i] = out[j * 4 + i] + qv[i] * vv[j]
            return tuple(out)

        acc = lax.fori_loop(0, 12, block, tuple(jnp.zeros((8, 128), F32) for _ in range(16)))
        for j in range(4):
            for i in range(4):
                ref[pl.ds(j * 8 + lead + i, 1), :] = jnp.sum(acc[j * 4 + i], axis=0, keepdims=True)

    def gram(ref, scale, pairs):
        used = sorted({a for a, _ in pairs} | {e for _, e in pairs})

        def block(b, acc):
            c, r = b // 4, pl.multiple_of((b % 4) * 16, 16)
            out = list(acc)
            for h in range(2):
                qv = {i: q[i, c, pl.ds(r + 8 * h, 8), :] for i in used}
                sv = qv
                if scale is not None:
                    weight = ij[scale, c, pl.ds(r + 8 * h, 8), :]
                    sv = {i: qv[i] * weight for i in {a for a, _ in pairs}}
                for n, (a, e) in enumerate(pairs):
                    out[n] = out[n] + sv[a] * qv[e]
            return tuple(out)

        acc = lax.fori_loop(0, 12, block, tuple(jnp.zeros((8, 128), F32) for _ in pairs))
        for n, (a, e) in enumerate(pairs):
            row = jnp.sum(acc[n], axis=0, keepdims=True)
            ref[pl.ds(a * 8 + e, 1), :] = row
            if a != e:
                ref[pl.ds(e * 8 + a, 1), :] = row

    def upper(first, second):
        return [(a, e) for a in first for e in second if a <= e]

    def lane_totals(block):
        return jnp.sum(block.T, axis=0, keepdims=True)

    def spread(row):
        return jnp.broadcast_to(row * (1.0 / dofs), (128, 128)).T

    def put_rows(planes, e, row):
        planes[e] = jnp.broadcast_to(row, (NS, 128))

    def row_sum(rbuf, e):
        return jnp.sum(rbuf[e], axis=0, keepdims=True)

    def own_rows(rbuf, e):
        return rbuf[e, pl.ds(pl.multiple_of(ri * NS, NS), NS), :]

    loads[0].wait()
    gather(q, 16)
    rm[pl.ds(96, 32), :] = jnp.zeros((32, 128), F32)
    half = (range(0, 4), range(4, 8))
    gram(rm.at[pl.ds(32, 64)], None, upper(half[0], half[0]))
    loads[1].wait()
    gather(u, 0)
    fold_dots(rm, u, 0)
    loads[2].wait()
    got = jnp.dot(jnp.concatenate(split2(dg[...]), axis=1), lsm[...], preferred_element_type=F32)
    spare_rows(0, 0, jnp.sum(got * rsm[...], axis=0, keepdims=True))
    spare_rows(0, 1, tgt)
    spare_rows(0, 2, jnp.full((1, 512), stiff, F32))
    spare_rows(0, 3, kpk)
    for j in range(4):
        spare_rows(16, j, jnp.zeros((1, 512), F32))
    for e in range(2):
        pa[e] = message(16 * e)
    splat = jnp.full((8, 128), stiff, F32)
    dgs[0] = jnp.concatenate([dg[48:64, :], splat], axis=0)
    dgs[1] = jnp.concatenate([dg[0:16, :], splat], axis=0)
    dg_edge = jnp.where(ri == 0, dg[pl.ds(15, 4, stride=16), :], dg[pl.ds(0, 4, stride=16), :])
    pack_radial(u, rsnd.at[0], dg_edge)
    pack_radial(q, rsnd.at[1], None)

    pl.semaphore_wait(barrier, len(OFFSETS) + 1)
    swap_q = send(q.at[pl.ds(0, 4)], q.at[pl.ds(4, 4)], twin)
    touched = exchange(pa, ra, (0, 2), (0, 0))
    halo_q = send_tangent(q.at[pl.ds(0, 4)], qt.at[:, pl.ds(0, 4)])
    halo_c = send_tangent(u, ut)
    halo_d = (send(dgs.at[0], dgt.at[0], nxt), send(dgs.at[1], dgt.at[1], prv))
    side_c = send(rsnd.at[0], ur, across)
    side_q = send(rsnd.at[1], qr.at[pl.ds(0, 4)], across)

    for j in range(4):
        for c in range(3):
            ij[j, c] = 1.0 / (stiff * 6.0 * kap[c, c] + dg[...] - shf[j])

    swap_q.wait_recv()
    fold_dots(rm, u, 1)
    gram(rm.at[pl.ds(32, 64)], None, upper(half[0], half[1]))
    gram(rm.at[pl.ds(32, 64)], None, upper(half[1], half[1]))
    put_rows(pa, 2, lane_totals(rm[pl.ds(0, 128), :]))
    summed = exchange(pa, ra, (2, 1), (2, 1))

    def weighted(j, carry):
        part = rm.at[pl.ds(pl.multiple_of(128 + j * 64, 64), 64)]
        for a, e in ((0, 0), (0, 1), (1, 1)):
            gram(part, j, upper(half[a], half[e]))
        return carry

    lax.fori_loop(0, 4, weighted, 0)
    for e in range(2):
        put_rows(pb, 2 + e, lane_totals(rm[pl.ds(128 + e * 128, 128), :]))

    for c in halo_d + halo_q + halo_c + (side_c, side_q):
        c.wait_recv()
    swap_t = send(qt.at[:, pl.ds(0, 4)], qt.at[:, pl.ds(4, 4)], twin)
    swap_r = send(qr.at[pl.ds(0, 4)], qr.at[pl.ds(4, 4)], twin)
    for side in range(2):
        sv = jnp.concatenate([dgt[side, 16:24, :], dgt[side, 16:24, :]], axis=0)
        dv = dgt[side, 0:16, :]
        for j in range(4):
            for c in range(3):
                ijt[side, j, c] = 1.0 / (sv * 6.0 * kap[c, c] + dv - shf[j])
    dv = ur[0, 12:16, :]
    base = jnp.concatenate([stiff * 6.0 * kap[c, c] + dv for c in range(3)] + [jnp.full((4, 128), 2.0, F32)], axis=0)
    for j in range(4):
        ijr[j] = 1.0 / (base - shf[j])

    touched()
    us[...] = unpack(own_rows(ra, 0))
    qs[pl.ds(0, 4)] = unpack(own_rows(ra, 1))
    swap_s = send(qs.at[pl.ds(0, 4)], qs.at[pl.ds(4, 4)], twin)
    dv = us[0, 12:16, :]
    sv = us[2, 12:16, :]
    base = jnp.concatenate([sv * 6.0 * kap[c, c] + dv for c in range(3)] + [jnp.full((4, 128), 2.0, F32)], axis=0)
    for j in range(4):
        ijs[j] = 1.0 / (base - shf[j])
    kr = us[3, 12:16, :]
    for sh in range(4):
        tv = us[1, 12 + sh : 13 + sh, :]
        tr = jnp.floor(tv * (1.0 / 128.0))
        tl = tv - 128.0 * tr
        lanes = slice(sh * 128, (sh + 1) * 128)
        rtm[:, lanes] = jnp.where(iota((64, 128), 0) == tr, 1.0, 0.0).astype(BF16)
        krow[pl.ds(sh, 1), :] = kr[sh : sh + 1, :]
        lands = jnp.where(iota((128, 128), 0) == tl, 1.0, 0.0).astype(BF16)
        ltm[:, lanes] = lands
        ltm[:, 512 + sh * 128 : 640 + sh * 128] = lands

    summed()
    wide = spread(row_sum(ra, 2))
    acf[...] = wide[0:32].reshape(4, 8, 128)
    st_s[...] = wide[32:96].reshape(8, 8, 128)

    def mix(coef, j, qv):
        n = qv[0].shape[0]
        acc = None
        for i in range(8):
            term = jnp.broadcast_to(coef[j, pl.ds(i, 1), :], (n, 128)) * qv[i]
            acc = term if acc is None else acc + term
        return acc

    regions = (
        (12, lambda b: (b // 4, pl.multiple_of((b % 4) * 16, 16)),
         lambda r, j, a: r[j, a[0], pl.ds(a[1], 16), :], (u, q, ij, d)),
        (6, lambda b: (b // 3, b % 3),
         lambda r, j, a: r[a[0], j, a[1]], (ut, qt, ijt, dt)),
        (1, lambda b: b, lambda r, j, a: r[j], (us, qs, ijs, ds)),
        (1, lambda b: b, lambda r, j, a: r[j], (ur, qr, ijr, dr)),
    )

    def put(region, j, a, v):
        if region == 0:
            u[j, a[0], pl.ds(a[1], 16), :] = v
        elif region == 1:
            ut[a[0], j, a[1]] = v
        elif region == 2:
            us[j] = v
        else:
            ur[j] = v

    def first_update(which):
        for n in which:
            blocks, place, get, (ru, rq, _, _) = regions[n]

            def step(b, carry):
                a = place(b)
                qv = [get(rq, i, a) for i in range(8)]
                for j in range(4):
                    put(n, j, a, get(ru, j, a) - mix(acf, j, qv))
                return carry

            lax.fori_loop(0, blocks, step, 0)

    def update(rnd):
        for n in range(4):
            blocks, place, get, (ru, rq, rj, rd) = regions[n]

            def step(b, carry):
                a = place(b)
                qv = [get(rq, i, a) for i in range(8)]
                for j in range(4):
                    new = get(ru, j, a) + DAMPING * get(rd.at[rnd], j, a)
                    new = new + get(rj, j, a) * mix(cf.at[0], j, qv) - mix(cf.at[1], j, qv)
                    put(n, j, a, new)
                return carry

            lax.fori_loop(0, blocks, step, 0)

    for c in halo_c:
        c.wait_send()
        pending[:] = [t for t in pending if t is not c]
    first_update((0,))
    swap_t.wait_recv()
    swap_r.wait_recv()
    swap_s.wait_recv()
    first_update((1, 2, 3))

    row_in = lax.broadcasted_iota(jnp.int32, (64, 128), 0) % 16
    lane_in = lax.broadcasted_iota(jnp.int32, (64, 128), 1)
    edge = row_in == 15 * (1 - ri)

    def apply(dref):
        def forces(j, carry):
            base = pl.multiple_of(j * 192, 192)
            for c in range(3):
                for sh in range(4):
                    v = us[j, pl.ds(c * 4 + sh, 1), :] * krow[pl.ds(sh, 1), :]
                    vh = v.astype(BF16).astype(F32)
                    mask = rtm[:, sh * 128 : (sh + 1) * 128]
                    for e, part in enumerate((vh, v - vh)):
                        full = jnp.broadcast_to(part, (64, 128)).astype(BF16)
                        amat[pl.ds(base + c * 64, 64), pl.ds(e * 512 + sh * 128, 128)] = mask * full
            return carry

        lax.fori_loop(0, 4, forces, 0)
        land[...] = lax.dot_general(amat[...], ltm[...], NT, preferred_element_type=F32)

        def column(j, carry):
            xs = [u[j, c] for c in range(3)]
            for c in range(3):
                v = xs[c]
                before = jnp.concatenate([ut[0, j, c], v[0:48]], axis=0)
                after = jnp.concatenate([v[16:64], ut[1, j, c]], axis=0)
                lap = 6.0 * v - before - after
                lap = lap - jnp.where(row_in == 0, 0.0, pltpu.roll(v, 1, 0))
                lap = lap - jnp.where(row_in == 15, 0.0, pltpu.roll(v, 63, 0))
                beside = jnp.concatenate(
                    [jnp.broadcast_to(ur[j, pl.ds(c * 4 + t, 1), :], (16, 128)) for t in range(4)], axis=0
                )
                lap = lap - jnp.where(edge, beside, 0.0)
                lap = lap - jnp.where(lane_in == 0, 0.0, pltpu.roll(v, 1, 1))
                lap = lap - jnp.where(lane_in == 127, 0.0, pltpu.roll(v, 127, 1))
                mixed = kap[c, c] * lap
                for e in range(3):
                    if e != c:
                        mixed = mixed + kap[c, e] * xs[e]
                out = stiff * mixed + (dg[...] - shf[j]) * v
                out = out + land[pl.ds(pl.multiple_of(j * 192, 192) + c * 64, 64), :]
                w[j, c] = out
                dref[j, c] = -(rho[j, c] + out) * ij[j, c]
            return carry

        lax.fori_loop(0, 4, column, 0)

    def coefficients(row, final):
        wide = spread(row)
        for j in range(4):
            b = wide[j * 8 : j * 8 + 8]
            e = wide[32 + j * 8 : 40 + j * 8]
            for i in range(8):
                e = e + mt_s[j, i] * b[i : i + 1, :]
            a = acf[j]
            if final:
                cf[0, j] = b
                cf[1, j] = a - DAMPING * e
            else:
                se = st_s[0] * e[0:1, :]
                for i in range(1, 8):
                    se = se + st_s[i] * e[i : i + 1, :]
                cf[0, j] = DAMPING * b
                cf[1, j] = DAMPING * (2.0 * e - se)
                acf[j] = a + DAMPING * (e - se)

    loads[3].wait()
    for rnd in range(3):
        last = rnd == 2
        dref = d.at[rnd]
        planes, rbuf = ((pb, rb), (pc, rc), (pd, rd))[rnd]
        apply(dref)
        if not last:
            pack_radial(dref, rsnd.at[2 + rnd], None)
            halo = send_tangent(dref, dt.at[rnd]) + (send(rsnd.at[2 + rnd], dr.at[rnd], across),)
            gather(dref, 0)
            planes[0] = message(0)
        for e in range(2):
            fold_dots(rm, w, e)
            fold_dots(rm.at[pl.ds(32, 32)], dref, e)
        put_rows(planes, 1, lane_totals(rm[pl.ds(0, 128), :]))
        nr = 3 if rnd == 0 else 1
        arrived = exchange(planes, rbuf, (1, 1) if last else (0, 1 + nr), (1, nr))
        if not last:
            for c in halo:
                c.wait_recv()
        arrived()
        if rnd == 0:
            for e in range(2):
                mt_s[pl.ds(2 * e, 2)] = spread(row_sum(rbuf, 2 + e)).reshape(2, 8, 8, 128)
        coefficients(row_sum(rbuf, 1), last)
        if not last:
            ds[rnd] = unpack(own_rows(rbuf, 0))
            update(rnd)

    def finish(b, carry):
        c, r = b // 4, pl.multiple_of((b % 4) * 16, 16)
        here = (c, pl.ds(r, 16))
        qv = [q[i, c, pl.ds(r, 16), :] for i in range(8)]
        for j in range(4):
            res = mix(cf.at[0], j, qv) - rho[j, c, pl.ds(r, 16), :] - w[j, c, pl.ds(r, 16), :]
            new = u[j, c, pl.ds(r, 16), :] + DAMPING * res * ij[j, c, pl.ds(r, 16), :] + mix(cf.at[1], j, qv)
            w[j, c, pl.ds(r, 16), :] = res
            rho[j, c, pl.ds(r, 16), :] = new
        return carry

    lax.fori_loop(0, 12, finish, 0)
    outs = [
        pltpu.make_async_copy(rho, oc_h, out_sem.at[0]),
        pltpu.make_async_copy(w, or_h, out_sem.at[1]),
    ]
    for c in outs:
        c.start()
    for c in pending:
        c.wait_send()
    for wait in drains:
        wait()
    for c in outs:
        c.wait()


def body(
    correction_guess, ritz_residual, ritz_basis, diagonal, coupling, class_ids,
    class_stiffness, shifts, contact_dest, contact_source, contact_target, contact_stiffness,
):
    cols, chans, tang, rloc, ax = correction_guess.shape
    devices = NX * NY * NZ * 2
    dofs = float(chans * tang * rloc * ax * devices)
    flat = (cols, chans, tang * rloc, ax)
    vm = pltpu.VMEM
    own = (4, 3, 64, 128)
    sheet = (4, 3, 16, 128)
    small = (4, 16, 128)
    scratch = [
        vm(own, F32), vm(own, F32), vm((8, 3, 64, 128), F32), vm((64, 128), F32), vm(own, F32), vm(own, F32),
        vm((3,) + own, F32),
        vm((2,) + sheet, F32), vm((2, 8, 3, 16, 128), F32), vm((2, 24, 128), F32), vm((2, 24, 128), F32),
        vm((2,) + sheet, F32), vm((2, 2) + sheet, F32),
        vm(small, F32), vm((8, 16, 128), F32), vm(small, F32), vm((2,) + small, F32),
        vm(small, F32), vm((8, 16, 128), F32), vm(small, F32), vm((2,) + small, F32), vm((4,) + small, F32),
        vm((256, 512), BF16), vm((64, 512), F32), vm((128, 1024), BF16), vm((64, 512), BF16), vm((32, 4, 128), F32),
        vm((768, 1024), BF16), vm((768, 128), F32), vm((8, 128), F32),
        vm((3, 64, 128), F32), vm((3, 128, 128), F32), vm((4, 64, 128), F32), vm((4, 128, 128), F32),
        vm((2, 64, 128), F32), vm((2, 128, 128), F32), vm((2, 64, 128), F32), vm((2, 128, 128), F32),
        vm((384, 128), F32),
        vm((2, 4, 8, 128), F32), vm((8, 8, 128), F32), vm((4, 8, 8, 128), F32), vm((4, 8, 128), F32),
        pltpu.SemaphoreType.DMA((4,)), pltpu.SemaphoreType.DMA((2,)),
        pltpu.SemaphoreType.DMA((36,)), pltpu.SemaphoreType.DMA((36,)),
    ]
    anyspace = pl.BlockSpec(memory_space=pl.ANY)
    smem = pl.BlockSpec(memory_space=pltpu.SMEM)
    correction, residual = pl.pallas_call(
        functools.partial(kernel, dofs),
        out_shape=(jax.ShapeDtypeStruct(flat, F32), jax.ShapeDtypeStruct(flat, F32)),
        in_specs=[pl.BlockSpec(memory_space=pltpu.VMEM)] * 4 + [smem] * 4 + [pl.BlockSpec(memory_space=pltpu.HBM)] * 4,
        out_specs=(anyspace, anyspace),
        scratch_shapes=scratch,
        compiler_params=pltpu.CompilerParams(collective_id=0, has_side_effects=True, vmem_limit_bytes=16 * 1024 * 1024),
        name="sweeps",
    )(
        contact_dest.reshape(2, 128), contact_source.reshape(2, 128), contact_target.reshape(2, 128),
        contact_stiffness.reshape(2, 128), coupling, class_ids, class_stiffness, shifts,
        *(pltpu.with_memory_space_constraint(a, pltpu.HBM) for a in (
            correction_guess.reshape(flat), ritz_residual.reshape(flat), ritz_basis.reshape(flat),
            diagonal.reshape(tang * rloc, ax),
        )),
    )
    shape = correction_guess.shape
    return correction.reshape(shape), residual.reshape(shape)


def solution(mesh):
    split = Mesh(
        mesh.devices.reshape(NX, NY, NZ, mesh.shape["radial"], mesh.shape["col"]),
        ("sector_0", "sector_1", "sector_2", "radial", "col"),
    )
    field = P("col", None, SECTOR, "radial", None)
    placed = (
        field, field, field, P(SECTOR, "radial", None), P(), P(SECTOR), P(), P("col"),
        P(SECTOR_RADIAL, None), P(SECTOR_RADIAL), P(SECTOR_RADIAL), P(SECTOR_RADIAL),
    )
    return jax.shard_map(body, mesh=split, in_specs=placed, out_specs=(field, field), check_vma=False)
```

```python
import functools

import jax
import jax.numpy as jnp
from jax import lax
from jax.experimental import pallas as pl
from jax.experimental.pallas import tpu as pltpu
from jax.sharding import Mesh
from jax.sharding import PartitionSpec as P

SECTOR = ("sector_0", "sector_1", "sector_2")
SECTOR_RADIAL = ("sector_0", "sector_1", "sector_2", "radial")
DAMPING = 0.7
NX, NY, NZ = 2, 4, 8
NS = NX * NY * NZ
SIZES = {"sector_0": NX, "sector_1": NY, "sector_2": NZ, "radial": 2}


def peer_offsets():
    along_x = {(0, 0): 0, (1, 0): 1, (0, 1): 2, (1, 1): 1}
    found = []
    for dr in range(2):
        for dx in range(NX):
            for dy in range(NY):
                for dz in range(NZ):
                    hops = along_x[dx, dr] + min(dy, NY - dy) + min(dz, NZ - dz)
                    steps = (("sector_0", dx), ("sector_1", dy), ("sector_2", dz), ("radial", dr))
                    if hops:
                        found.append((-hops, tuple(t for t in steps if t[1])))
    return [t[1] for t in sorted(found, key=lambda t: t[0])]


OFFSETS = peer_offsets()
F32 = jnp.float32
BF16 = jnp.bfloat16
MESH_ID = pl.DeviceIdType.MESH
NT = (((1,), (1,)), ((), ()))


def split2(x):
    hi = x.astype(BF16)
    return hi, (x - hi.astype(F32)).astype(BF16)


def iota(shape, dim):
    return lax.broadcasted_iota(jnp.int32, shape, dim).astype(F32)


def kernel(
    dofs,
    dst_r, src_r, tgt_r, kst_r, kap, cid, cst, shf, c0_h, rho_h, q_h, dg_h,
    oc_h, or_h,
    u, rho, q, dg, ij, w, d,
    ut, qt, dgt, dgs, ijt, dt,
    us, qs, ijs, ds,
    ur, qr, ijr, dr, rsnd,
    lsm, rsm, ltm, rtm, wbuf, amat, land, krow,
    pa, ra, pb, rb, pc, rc, pd, rd,
    rm,
    cf, st_s, mt_s, acf,
    ld_sem, snd, rcv,
):
    x = lax.axis_index("sector_0")
    y = lax.axis_index("sector_1")
    z = lax.axis_index("sector_2")
    ri = lax.axis_index("radial")
    me_col = lax.axis_index("col")

    here = {"sector_0": x, "sector_1": y, "sector_2": z, "radial": ri}

    def peer(offset):
        place = {}
        for name, step in offset:
            at = here[name] + step
            place[name] = jnp.where(at >= SIZES[name], at - SIZES[name], at)
        return place

    def sector_of(place):
        return (place.get("sector_0", x) * NY + place.get("sector_1", y)) * NZ + place.get("sector_2", z)

    me = sector_of({})
    me_row = ri * NS + me

    c1 = (z + 1) // NZ
    c2 = (y + c1) // NY
    nxt = {"sector_2": (z + 1) % NZ, "sector_1": (y + c1) % NY, "sector_0": (x + c2) % NX}
    b1 = 1 - (z + NZ - 1) // NZ
    b2 = 1 - (y + NY - b1) // NY
    prv = {"sector_2": (z + NZ - 1) % NZ, "sector_1": (y + NY - b1) % NY, "sector_0": (x + NX - b2) % NX}
    across = {"radial": 1 - ri}
    twin = {"col": 1 - me_col}

    barrier = pltpu.get_barrier_semaphore()

    def sig(dev):
        pl.semaphore_signal(barrier, inc=1, device_id=dev, device_id_type=MESH_ID)

    loads = [
        pltpu.make_async_copy(q_h, q.at[pl.ds(0, 4)], ld_sem.at[0]),
        pltpu.make_async_copy(c0_h, u, ld_sem.at[1]),
        pltpu.make_async_copy(dg_h, dg, ld_sem.at[2]),
        pltpu.make_async_copy(rho_h, rho, ld_sem.at[3]),
    ]
    for c in loads:
        c.start()

    for offset in OFFSETS:
        sig(peer(offset))
    sig(twin)

    count = [0]
    pending = []

    def rcopy(src, dst, dev, idx, kind=MESH_ID):
        return pltpu.make_async_remote_copy(
            src_ref=src, dst_ref=dst, send_sem=snd.at[idx], recv_sem=rcv.at[idx],
            device_id=dev, device_id_type=kind,
        )

    def send(src, dst, dev):
        idx = count[0]
        count[0] += 1
        c = rcopy(src, dst, dev, idx)
        c.start()
        pending.append(c)
        return c

    def exchange(planes, rbuf, same, other):
        (a0, an), (b0, bn) = same, other
        idx = count[0]
        count[0] += 2
        for offset in OFFSETS:
            place = peer(offset)
            across_slab = "radial" in place
            first, num = (b0, bn) if across_slab else (a0, an)
            if num == 0:
                continue
            row = sector_of(place)
            rcopy(
                planes.at[pl.ds(first, num), pl.ds(row, 1)],
                rbuf.at[pl.ds(first, num), pl.ds(me_row, 1)],
                place, idx + int(across_slab),
            ).start()
        for e in range(a0, a0 + an):
            rbuf[e, pl.ds(me_row, 1), :] = planes[e, pl.ds(me, 1), :]

        def finish(sem):
            if an:
                part = rbuf.at[pl.ds(a0, an), pl.ds(0, NS - 1)]
                pltpu.make_async_copy(part, part, sem.at[idx]).wait()
            if bn:
                part = rbuf.at[pl.ds(b0, bn), pl.ds(0, NS)]
                pltpu.make_async_copy(part, part, sem.at[idx + 1]).wait()

        drains.append(lambda: finish(snd))
        return lambda: finish(rcv)

    drains = []

    stiff = cst[cid[0]]

    meta = [r[...].astype(F32) for r in (dst_r, src_r, tgt_r, kst_r)]

    def flat_row(m):
        return jnp.concatenate([m[0:1, :], m[1:2, :]], axis=1)

    dest = flat_row(meta[0])
    later = iota((128, 256), 1)
    rank = jnp.zeros((1, 256), F32)
    for h in range(2):
        column = jnp.broadcast_to(meta[0][h : h + 1, :], (128, 128)).T
        column = jnp.concatenate([column, column], axis=1)
        hit = (column == dest) & (iota((128, 256), 0) + 128.0 * h < later)
        rank = rank + jnp.sum(jnp.where(hit, 1.0, 0.0), axis=0, keepdims=True)
    slot = rank * 64.0 + dest
    source, target, kst = flat_row(meta[1]), flat_row(meta[2]), flat_row(meta[3])
    s_row = jnp.floor(source * (1.0 / 128.0))
    t_row = jnp.floor(target * (1.0 / 128.0))
    k_hi = kst.astype(BF16).astype(F32)
    k_mid = (kst - k_hi).astype(BF16).astype(F32)
    k_lo = kst - k_hi - k_mid
    rows = jnp.concatenate(
        [s_row, source - 128.0 * s_row, t_row, target - 128.0 * t_row, k_hi, k_mid, k_lo, jnp.ones((1, 256), F32)],
        axis=0,
    ).astype(BF16)
    onehot = jnp.where(iota((512, 256), 0) == slot, 1.0, 0.0).astype(BF16)
    packed = lax.dot_general(rows, onehot, NT, preferred_element_type=F32)
    valid = packed[7:8, :] > 0.5
    src_row = jnp.where(valid, packed[0:1, :], -1.0)
    picks = jnp.where(iota((128, 512), 0) == packed[1:2, :], 1.0, 0.0).astype(BF16)
    lsm[...] = jnp.concatenate([picks, picks], axis=0)
    rsm[...] = jnp.where(iota((64, 512), 0) == src_row, 1.0, 0.0)
    tgt = packed[2:3, :] * 128.0 + packed[3:4, :]
    kpk = packed[4:5, :] + packed[5:6, :] + packed[6:7, :]

    def edge_rows(ref, j, c):
        top = ref[j, c, pl.ds(15, 4, stride=16), :]
        bottom = ref[j, c, pl.ds(0, 4, stride=16), :]
        return jnp.where(ri == 0, top, bottom)

    def pack_radial(ref, out, spare):
        for j in range(4):
            tail = spare if (spare is not None and j == 0) else jnp.zeros((4, 128), F32)
            out[j] = jnp.concatenate([edge_rows(ref, j, c) for c in range(3)] + [tail], axis=0)

    def send_tangent(ref, dst):
        a = send(ref.at[:, :, pl.ds(48, 16), :], dst.at[0], nxt)
        b = send(ref.at[:, :, pl.ds(0, 16), :], dst.at[1], prv)
        return a, b

    def gather(ref, base):
        def column(j, carry):
            xs = jnp.concatenate([ref[j, c] for c in range(3)], axis=0)
            both = jnp.concatenate(split2(xs), axis=1)
            got = jnp.dot(both, lsm[...], preferred_element_type=F32)
            for c in range(3):
                picked = jnp.sum(got[c * 64 : (c + 1) * 64] * rsm[...], axis=0, keepdims=True)
                for sh in range(4):
                    wbuf[base + j * 4 + c, pl.ds(sh, 1), :] = picked[:, sh * 128 : (sh + 1) * 128]
            return carry

        for j in range(4):
            column(j, 0)

    def spare_rows(base, j, row):
        for sh in range(4):
            wbuf[base + j * 4 + 3, pl.ds(sh, 1), :] = row[:, sh * 128 : (sh + 1) * 128]

    def message(base):
        m = wbuf[pl.ds(base, 16)].reshape(64, 128)
        turned = jnp.concatenate([m, m], axis=0).T
        lane = lax.broadcasted_iota(jnp.int32, (64, 128), 1)
        return jnp.where(lane < 64, turned[0:64], turned[64:128])

    def unpack(m):
        both = jnp.concatenate([m, pltpu.roll(m, 64, 1)], axis=0).T
        return both[0:64].reshape(4, 16, 128)

    def fold_dots(ref, vref, half):
        lead = half * 4

        def block(c, acc):
            out = list(acc)
            for e in range(8):
                qv = [q[lead + i, c, 8 * e : 8 * e + 8, :] for i in range(4)]
                vv = [vref[j, c, 8 * e : 8 * e + 8, :] for j in range(4)]
                for j in range(4):
                    for i in range(4):
                        out[j * 4 + i] = out[j * 4 + i] + qv[i] * vv[j]
            return tuple(out)

        acc = lax.fori_loop(0, 3, block, tuple(jnp.zeros((8, 128), F32) for _ in range(16)))
        for j in range(4):
            for i in range(4):
                ref[pl.ds(j * 8 + lead + i, 1), :] = jnp.sum(acc[j * 4 + i], axis=0, keepdims=True)

    def gram(ref, scale, pairs):
        used = sorted({a for a, _ in pairs} | {e for _, e in pairs})

        def block(b, acc):
            c, r = b // 2, pl.multiple_of((b % 2) * 32, 32)
            out = list(acc)
            for h in range(4):
                qv = {i: q[i, c, pl.ds(r + 8 * h, 8), :] for i in used}
                sv = qv
                if scale is not None:
                    weight = ij[scale, c, pl.ds(r + 8 * h, 8), :]
                    sv = {i: qv[i] * weight for i in {a for a, _ in pairs}}
                for n, (a, e) in enumerate(pairs):
                    out[n] = out[n] + sv[a] * qv[e]
            return tuple(out)

        acc = lax.fori_loop(0, 6, block, tuple(jnp.zeros((8, 128), F32) for _ in pairs))
        for n, (a, e) in enumerate(pairs):
            row = jnp.sum(acc[n], axis=0, keepdims=True)
            ref[pl.ds(a * 8 + e, 1), :] = row
            if a != e:
                ref[pl.ds(e * 8 + a, 1), :] = row

    def upper(first, second):
        return [(a, e) for a in first for e in second if a <= e]

    def lane_totals(block):
        return jnp.sum(block.T, axis=0, keepdims=True)

    def spread(row):
        return jnp.broadcast_to(row * (1.0 / dofs), (128, 128)).T

    def put_rows(planes, e, row):
        planes[e] = jnp.broadcast_to(row, (NS, 128))

    def row_sum(rbuf, e):
        return jnp.sum(rbuf[e], axis=0, keepdims=True)

    def own_rows(rbuf, e):
        return rbuf[e, pl.ds(pl.multiple_of(ri * NS, NS), NS), :]

    loads[0].wait()
    gather(q, 16)
    rm[pl.ds(96, 32), :] = jnp.zeros((32, 128), F32)
    half = (range(0, 4), range(4, 8))
    gram(rm.at[pl.ds(32, 64)], None, upper(half[0], half[0]))
    loads[1].wait()
    gather(u, 0)
    fold_dots(rm, u, 0)
    loads[2].wait()
    got = jnp.dot(jnp.concatenate(split2(dg[...]), axis=1), lsm[...], preferred_element_type=F32)
    spare_rows(0, 0, jnp.sum(got * rsm[...], axis=0, keepdims=True))
    spare_rows(0, 1, tgt)
    spare_rows(0, 2, jnp.full((1, 512), stiff, F32))
    spare_rows(0, 3, kpk)
    for j in range(4):
        spare_rows(16, j, jnp.zeros((1, 512), F32))
    for e in range(2):
        pa[e] = message(16 * e)
    splat = jnp.full((8, 128), stiff, F32)
    dgs[0] = jnp.concatenate([dg[48:64, :], splat], axis=0)
    dgs[1] = jnp.concatenate([dg[0:16, :], splat], axis=0)
    dg_edge = jnp.where(ri == 0, dg[pl.ds(15, 4, stride=16), :], dg[pl.ds(0, 4, stride=16), :])
    pack_radial(u, rsnd.at[0], dg_edge)
    pack_radial(q, rsnd.at[1], None)

    pl.semaphore_wait(barrier, len(OFFSETS) + 1)
    swap_q = send(q.at[pl.ds(0, 4)], q.at[pl.ds(4, 4)], twin)
    touched = exchange(pa, ra, (0, 2), (0, 0))
    halo_c = send_tangent(u, ut)

    for j in range(4):
        for c in range(3):
            ij[j, c] = 1.0 / (stiff * 6.0 * kap[c, c] + dg[...] - shf[j])

    swap_q.wait_recv()
    fold_dots(rm, u, 1)
    gram(rm.at[pl.ds(32, 64)], None, upper(half[0], half[1]))
    gram(rm.at[pl.ds(32, 64)], None, upper(half[1], half[1]))
    put_rows(pa, 2, lane_totals(rm[pl.ds(0, 128), :]))
    summed = exchange(pa, ra, (2, 1), (2, 1))
    halo_q = send_tangent(q.at[pl.ds(0, 4)], qt.at[:, pl.ds(0, 4)])
    halo_d = (send(dgs.at[0], dgt.at[0], nxt), send(dgs.at[1], dgt.at[1], prv))
    side_c = send(rsnd.at[0], ur, across)
    side_q = send(rsnd.at[1], qr.at[pl.ds(0, 4)], across)

    def weighted(j, carry):
        part = rm.at[pl.ds(pl.multiple_of(128 + j * 64, 64), 64)]
        for a, e in ((0, 0), (0, 1), (1, 1)):
            gram(part, j, upper(half[a], half[e]))
        return carry

    lax.fori_loop(0, 4, weighted, 0)
    for e in range(2):
        put_rows(pb, 2 + e, lane_totals(rm[pl.ds(128 + e * 128, 128), :]))

    for c in halo_d + halo_q + halo_c + (side_c, side_q):
        c.wait_recv()
    swap_t = send(qt.at[:, pl.ds(0, 4)], qt.at[:, pl.ds(4, 4)], twin)
    swap_r = send(qr.at[pl.ds(0, 4)], qr.at[pl.ds(4, 4)], twin)
    for side in range(2):
        sv = jnp.concatenate([dgt[side, 16:24, :], dgt[side, 16:24, :]], axis=0)
        dv = dgt[side, 0:16, :]
        for j in range(4):
            for c in range(3):
                ijt[side, j, c] = 1.0 / (sv * 6.0 * kap[c, c] + dv - shf[j])
    dv = ur[0, 12:16, :]
    base = jnp.concatenate([stiff * 6.0 * kap[c, c] + dv for c in range(3)] + [jnp.full((4, 128), 2.0, F32)], axis=0)
    for j in range(4):
        ijr[j] = 1.0 / (base - shf[j])

    touched()
    us[...] = unpack(own_rows(ra, 0))
    qs[pl.ds(0, 4)] = unpack(own_rows(ra, 1))
    swap_s = send(qs.at[pl.ds(0, 4)], qs.at[pl.ds(4, 4)], twin)
    dv = us[0, 12:16, :]
    sv = us[2, 12:16, :]
    base = jnp.concatenate([sv * 6.0 * kap[c, c] + dv for c in range(3)] + [jnp.full((4, 128), 2.0, F32)], axis=0)
    for j in range(4):
        ijs[j] = 1.0 / (base - shf[j])
    kr = us[3, 12:16, :]
    for sh in range(4):
        tv = us[1, 12 + sh : 13 + sh, :]
        tr = jnp.floor(tv * (1.0 / 128.0))
        tl = tv - 128.0 * tr
        lanes = slice(sh * 128, (sh + 1) * 128)
        rtm[:, lanes] = jnp.where(iota((64, 128), 0) == tr, 1.0, 0.0).astype(BF16)
        krow[pl.ds(sh, 1), :] = kr[sh : sh + 1, :]
        lands = jnp.where(iota((128, 128), 0) == tl, 1.0, 0.0).astype(BF16)
        ltm[:, lanes] = lands
        ltm[:, 512 + sh * 128 : 640 + sh * 128] = lands

    summed()
    wide = spread(row_sum(ra, 2))
    acf[...] = wide[0:32].reshape(4, 8, 128)
    st_s[...] = wide[32:96].reshape(8, 8, 128)

    def mix(coef, j, qv):
        n = qv[0].shape[0]
        acc = None
        for i in range(8):
            term = jnp.broadcast_to(coef[j, pl.ds(i, 1), :], (n, 128)) * qv[i]
            acc = term if acc is None else acc + term
        return acc

    regions = (
        (12, lambda b: (b // 4, pl.multiple_of((b % 4) * 16, 16)),
         lambda r, j, a: r[j, a[0], pl.ds(a[1], 16), :], (u, q, ij, d)),
        (6, lambda b: (b // 3, b % 3),
         lambda r, j, a: r[a[0], j, a[1]], (ut, qt, ijt, dt)),
        (1, lambda b: b, lambda r, j, a: r[j], (us, qs, ijs, ds)),
        (1, lambda b: b, lambda r, j, a: r[j], (ur, qr, ijr, dr)),
    )

    def put(region, j, a, v):
        if region == 0:
            u[j, a[0], pl.ds(a[1], 16), :] = v
        elif region == 1:
            ut[a[0], j, a[1]] = v
        elif region == 2:
            us[j] = v
        else:
            ur[j] = v

    def first_update(which):
        for n in which:
            blocks, place, get, (ru, rq, _, _) = regions[n]

            def step(b, carry):
                a = place(b)
                qv = [get(rq, i, a) for i in range(8)]
                for j in range(4):
                    put(n, j, a, get(ru, j, a) - mix(acf, j, qv))
                return carry

            lax.fori_loop(0, blocks, step, 0)

    def update(rnd, which):
        for n in which:
            blocks, place, get, (ru, rq, rj, rd) = regions[n]

            def step(b, carry):
                a = place(b)
                qv = [get(rq, i, a) for i in range(8)]
                for j in range(4):
                    new = get(ru, j, a) + DAMPING * get(rd.at[rnd], j, a)
                    new = new + get(rj, j, a) * mix(cf.at[0], j, qv) - mix(cf.at[1], j, qv)
                    put(n, j, a, new)
                return carry

            lax.fori_loop(0, blocks, step, 0)

    for c in halo_c:
        c.wait_send()
        pending[:] = [t for t in pending if t is not c]
    first_update((0,))
    swap_t.wait_recv()
    swap_r.wait_recv()
    swap_s.wait_recv()
    first_update((1, 2, 3))

    row_in = lax.broadcasted_iota(jnp.int32, (64, 128), 0) % 16
    lane_in = lax.broadcasted_iota(jnp.int32, (64, 128), 1)
    edge = row_in == 15 * (1 - ri)

    def apply(dref):
        def forces(j, carry):
            base = pl.multiple_of(j * 192, 192)
            for c in range(3):
                vs = us[j, c * 4 : c * 4 + 4, :] * krow[0:4, :]
                vh = vs.astype(BF16).astype(F32)
                for sh in range(4):
                    mask = rtm[:, sh * 128 : (sh + 1) * 128]
                    for e, part in enumerate((vh, vs - vh)):
                        full = jnp.broadcast_to(part[sh : sh + 1, :], (16, 128)).astype(BF16)
                        for t in range(4):
                            amat[pl.ds(base + c * 64 + 16 * t, 16), pl.ds(e * 512 + sh * 128, 128)] = (
                                mask[16 * t : 16 * t + 16] * full
                            )
            return carry

        lax.fori_loop(0, 4, forces, 0)
        land[...] = lax.dot_general(amat[...], ltm[...], NT, preferred_element_type=F32)

        def column(j, carry):
            xs = [u[j, c] for c in range(3)]
            for c in range(3):
                v = xs[c]
                before = jnp.concatenate([ut[0, j, c], v[0:48]], axis=0)
                after = jnp.concatenate([v[16:64], ut[1, j, c]], axis=0)
                lap = 6.0 * v - before - after
                lap = lap - jnp.where(row_in == 0, 0.0, pltpu.roll(v, 1, 0))
                lap = lap - jnp.where(row_in == 15, 0.0, pltpu.roll(v, 63, 0))
                beside = jnp.concatenate(
                    [jnp.broadcast_to(ur[j, pl.ds(c * 4 + t, 1), :], (16, 128)) for t in range(4)], axis=0
                )
                lap = lap - jnp.where(edge, beside, 0.0)
                lap = lap - jnp.where(lane_in == 0, 0.0, pltpu.roll(v, 1, 1))
                lap = lap - jnp.where(lane_in == 127, 0.0, pltpu.roll(v, 127, 1))
                mixed = kap[c, c] * lap
                for e in range(3):
                    if e != c:
                        mixed = mixed + kap[c, e] * xs[e]
                out = stiff * mixed + (dg[...] - shf[j]) * v
                out = out + land[pl.ds(pl.multiple_of(j * 192, 192) + c * 64, 64), :]
                w[j, c] = out
                dref[j, c] = -(rho[j, c] + out) * ij[j, c]
            return carry

        lax.fori_loop(0, 4, column, 0)

    def coefficients(row, final):
        wide = spread(row)
        for j in range(4):
            b = wide[j * 8 : j * 8 + 8]
            e = wide[32 + j * 8 : 40 + j * 8]
            for i in range(8):
                e = e + mt_s[j, i] * b[i : i + 1, :]
            a = acf[j]
            if final:
                cf[0, j] = b
                cf[1, j] = a - DAMPING * e
            else:
                se = st_s[0] * e[0:1, :]
                for i in range(1, 8):
                    se = se + st_s[i] * e[i : i + 1, :]
                cf[0, j] = DAMPING * b
                cf[1, j] = DAMPING * (2.0 * e - se)
                acf[j] = a + DAMPING * (e - se)

    loads[3].wait()
    for rnd in range(3):
        last = rnd == 2
        dref = d.at[rnd]
        planes, rbuf = ((pb, rb), (pc, rc), (pd, rd))[rnd]
        apply(dref)
        for e in range(2):
            fold_dots(rm, w, e)
            fold_dots(rm.at[pl.ds(32, 32)], dref, e)
        put_rows(planes, 1, lane_totals(rm[pl.ds(0, 128), :]))
        nr = 3 if rnd == 0 else 1
        summed = exchange(planes, rbuf, (1, nr), (1, nr))
        if not last:
            gather(dref, 0)
            planes[0] = message(0)
            touched = exchange(planes, rbuf, (0, 1), (0, 0))
            pack_radial(dref, rsnd.at[2 + rnd], None)
            halo = send_tangent(dref, dt.at[rnd]) + (send(rsnd.at[2 + rnd], dr.at[rnd], across),)
        summed()
        if rnd == 0:
            for e in range(2):
                mt_s[pl.ds(2 * e, 2)] = spread(row_sum(rbuf, 2 + e)).reshape(2, 8, 8, 128)
        coefficients(row_sum(rbuf, 1), last)
        if not last:
            update(rnd, (0,))
            for c in halo:
                c.wait_recv()
            update(rnd, (1, 3))
            touched()
            ds[rnd] = unpack(own_rows(rbuf, 0))
            update(rnd, (2,))

    def finish(b, carry):
        c, r = b // 4, pl.multiple_of((b % 4) * 16, 16)
        here = (c, pl.ds(r, 16))
        qv = [q[i, c, pl.ds(r, 16), :] for i in range(8)]
        for j in range(4):
            res = mix(cf.at[0], j, qv) - rho[j, c, pl.ds(r, 16), :] - w[j, c, pl.ds(r, 16), :]
            new = u[j, c, pl.ds(r, 16), :] + DAMPING * res * ij[j, c, pl.ds(r, 16), :] + mix(cf.at[1], j, qv)
            or_h[j, c, pl.ds(r, 16), :] = res
            oc_h[j, c, pl.ds(r, 16), :] = new
        return carry

    lax.fori_loop(0, 12, finish, 0)
    for c in pending:
        c.wait_send()
    for wait in drains:
        wait()


def store(a, b, out_a, out_b, sem):
    copies = [pltpu.make_async_copy(a, out_a, sem.at[0]), pltpu.make_async_copy(b, out_b, sem.at[1])]
    for c in copies:
        c.start()
    for c in copies:
        c.wait()


def in_hbm(a):
    return pltpu.with_memory_space_constraint(a, pltpu.HBM)


def body(
    correction_guess, ritz_residual, ritz_basis, diagonal, coupling, class_ids,
    class_stiffness, shifts, contact_dest, contact_source, contact_target, contact_stiffness,
):
    cols, chans, tang, rloc, ax = correction_guess.shape
    devices = NX * NY * NZ * 2
    dofs = float(chans * tang * rloc * ax * devices)
    flat = (cols, chans, tang * rloc, ax)
    vm = pltpu.VMEM
    own = (4, 3, 64, 128)
    sheet = (4, 3, 16, 128)
    small = (4, 16, 128)
    scratch = [
        vm(own, F32), vm(own, F32), vm((8, 3, 64, 128), F32), vm((64, 128), F32), vm(own, F32), vm(own, F32),
        vm((3,) + own, F32),
        vm((2,) + sheet, F32), vm((2, 8, 3, 16, 128), F32), vm((2, 24, 128), F32), vm((2, 24, 128), F32),
        vm((2,) + sheet, F32), vm((2, 2) + sheet, F32),
        vm(small, F32), vm((8, 16, 128), F32), vm(small, F32), vm((2,) + small, F32),
        vm(small, F32), vm((8, 16, 128), F32), vm(small, F32), vm((2,) + small, F32), vm((4,) + small, F32),
        vm((256, 512), BF16), vm((64, 512), F32), vm((128, 1024), BF16), vm((64, 512), BF16), vm((32, 4, 128), F32),
        vm((768, 1024), BF16), vm((768, 128), F32), vm((8, 128), F32),
        vm((3, 64, 128), F32), vm((3, 128, 128), F32), vm((4, 64, 128), F32), vm((4, 128, 128), F32),
        vm((2, 64, 128), F32), vm((2, 128, 128), F32), vm((2, 64, 128), F32), vm((2, 128, 128), F32),
        vm((384, 128), F32),
        vm((2, 4, 8, 128), F32), vm((8, 8, 128), F32), vm((4, 8, 8, 128), F32), vm((4, 8, 128), F32),
        pltpu.SemaphoreType.DMA((4,)),
        pltpu.SemaphoreType.DMA((36,)), pltpu.SemaphoreType.DMA((36,)),
    ]
    anyspace = pl.BlockSpec(memory_space=pl.ANY)
    smem = pl.BlockSpec(memory_space=pltpu.SMEM)
    correction, residual = pl.pallas_call(
        functools.partial(kernel, dofs),
        out_shape=(jax.ShapeDtypeStruct(flat, F32), jax.ShapeDtypeStruct(flat, F32)),
        in_specs=[pl.BlockSpec(memory_space=pltpu.VMEM)] * 4 + [smem] * 4 + [anyspace] * 4,
        out_specs=(pl.BlockSpec(memory_space=pltpu.VMEM),) * 2,
        scratch_shapes=scratch,
        compiler_params=pltpu.CompilerParams(collective_id=0, has_side_effects=True, vmem_limit_bytes=16 * 1024 * 1024),
        name="sweeps",
    )(
        contact_dest.reshape(2, 128), contact_source.reshape(2, 128), contact_target.reshape(2, 128),
        contact_stiffness.reshape(2, 128), coupling, class_ids, class_stiffness, shifts,
        in_hbm(correction_guess.reshape(flat)), in_hbm(ritz_residual.reshape(flat)),
        in_hbm(ritz_basis.reshape(flat)), in_hbm(diagonal.reshape(tang * rloc, ax)),
    )
    correction, residual = pl.pallas_call(
        store,
        out_shape=(jax.ShapeDtypeStruct(flat, F32), jax.ShapeDtypeStruct(flat, F32)),
        in_specs=[anyspace] * 2,
        out_specs=(anyspace, anyspace),
        scratch_shapes=[pltpu.SemaphoreType.DMA((2,))],
        compiler_params=pltpu.CompilerParams(vmem_limit_bytes=1024 * 1024),
        name="store",
    )(correction, residual)
    shape = correction_guess.shape
    return correction.reshape(shape), residual.reshape(shape)


def solution(mesh):
    split = Mesh(
        mesh.devices.reshape(NX, NY, NZ, mesh.shape["radial"], mesh.shape["col"]),
        ("sector_0", "sector_1", "sector_2", "radial", "col"),
    )
    field = P("col", None, SECTOR, "radial", None)
    placed = (
        field, field, field, P(SECTOR, "radial", None), P(), P(SECTOR), P(), P("col"),
        P(SECTOR_RADIAL, None), P(SECTOR_RADIAL), P(SECTOR_RADIAL), P(SECTOR_RADIAL),
    )
    return jax.shard_map(body, mesh=split, in_specs=placed, out_specs=(field, field), check_vma=False)
```

```python
import functools

import jax
import jax.numpy as jnp
from jax import lax
from jax.experimental import pallas as pl
from jax.experimental.pallas import tpu as pltpu
from jax.sharding import Mesh
from jax.sharding import PartitionSpec as P

SECTOR = ("sector_0", "sector_1", "sector_2")
SECTOR_RADIAL = ("sector_0", "sector_1", "sector_2", "radial")
DAMPING = 0.7
NX, NY, NZ = 2, 4, 8
NS = NX * NY * NZ
SIZES = {"sector_0": NX, "sector_1": NY, "sector_2": NZ, "radial": 2}


def peer_offsets():
    along_x = {(0, 0): 0, (1, 0): 1, (0, 1): 2, (1, 1): 1}
    found = []
    for dr in range(2):
        for dx in range(NX):
            for dy in range(NY):
                for dz in range(NZ):
                    hops = along_x[dx, dr] + min(dy, NY - dy) + min(dz, NZ - dz)
                    steps = (("sector_0", dx), ("sector_1", dy), ("sector_2", dz), ("radial", dr))
                    if hops:
                        found.append((-hops, tuple(t for t in steps if t[1])))
    return [t[1] for t in sorted(found, key=lambda t: t[0])]


OFFSETS = peer_offsets()
F32 = jnp.float32
BF16 = jnp.bfloat16
MESH_ID = pl.DeviceIdType.MESH
NT = (((1,), (1,)), ((), ()))


def split2(x):
    hi = x.astype(BF16)
    return hi, (x - hi.astype(F32)).astype(BF16)


def iota(shape, dim):
    return lax.broadcasted_iota(jnp.int32, shape, dim).astype(F32)


def kernel(
    dofs,
    dst_r, src_r, tgt_r, kst_r, kap, cid, cst, shf, c0_h, rho_h, q_h, dg_h,
    oc_h, or_h,
    u, rho, q, dg, ij, w, d,
    ut, qt, dgt, dgs, ijt, dt,
    us, qs, ijs, ds,
    ur, qr, ijr, dr, rsnd,
    lsm, rsm, ltm, rtm, wbuf, amat, land, krow,
    pa, ra, pb, rb, pc, rc, pd, rd,
    rm,
    cf, st_s, mt_s, acf,
    ld_sem, snd, rcv,
):
    x = lax.axis_index("sector_0")
    y = lax.axis_index("sector_1")
    z = lax.axis_index("sector_2")
    ri = lax.axis_index("radial")
    me_col = lax.axis_index("col")

    here = {"sector_0": x, "sector_1": y, "sector_2": z, "radial": ri}

    def peer(offset):
        place = {}
        for name, step in offset:
            at = here[name] + step
            place[name] = jnp.where(at >= SIZES[name], at - SIZES[name], at)
        return place

    def sector_of(place):
        return (place.get("sector_0", x) * NY + place.get("sector_1", y)) * NZ + place.get("sector_2", z)

    me = sector_of({})
    me_row = ri * NS + me

    c1 = (z + 1) // NZ
    c2 = (y + c1) // NY
    nxt = {"sector_2": (z + 1) % NZ, "sector_1": (y + c1) % NY, "sector_0": (x + c2) % NX}
    b1 = 1 - (z + NZ - 1) // NZ
    b2 = 1 - (y + NY - b1) // NY
    prv = {"sector_2": (z + NZ - 1) % NZ, "sector_1": (y + NY - b1) % NY, "sector_0": (x + NX - b2) % NX}
    across = {"radial": 1 - ri}
    twin = {"col": 1 - me_col}

    barrier = pltpu.get_barrier_semaphore()

    def sig(dev):
        pl.semaphore_signal(barrier, inc=1, device_id=dev, device_id_type=MESH_ID)

    loads = [
        pltpu.make_async_copy(q_h, q.at[pl.ds(0, 4)], ld_sem.at[0]),
        pltpu.make_async_copy(c0_h, u, ld_sem.at[1]),
        pltpu.make_async_copy(dg_h, dg, ld_sem.at[2]),
        pltpu.make_async_copy(rho_h, rho, ld_sem.at[3]),
    ]
    for c in loads:
        c.start()

    for offset in OFFSETS:
        sig(peer(offset))
    sig(twin)

    count = [0]
    pending = []

    def rcopy(src, dst, dev, idx, kind=MESH_ID):
        return pltpu.make_async_remote_copy(
            src_ref=src, dst_ref=dst, send_sem=snd.at[idx], recv_sem=rcv.at[idx],
            device_id=dev, device_id_type=kind,
        )

    def send(src, dst, dev):
        idx = count[0]
        count[0] += 1
        c = rcopy(src, dst, dev, idx)
        c.start()
        pending.append(c)
        return c

    def exchange(planes, rbuf, same, other):
        (a0, an), (b0, bn) = same, other
        idx = count[0]
        count[0] += 2
        for offset in OFFSETS:
            place = peer(offset)
            across_slab = "radial" in place
            first, num = (b0, bn) if across_slab else (a0, an)
            if num == 0:
                continue
            row = sector_of(place)
            rcopy(
                planes.at[pl.ds(first, num), pl.ds(row, 1)],
                rbuf.at[pl.ds(first, num), pl.ds(me_row, 1)],
                place, idx + int(across_slab),
            ).start()
        for e in range(a0, a0 + an):
            rbuf[e, pl.ds(me_row, 1), :] = planes[e, pl.ds(me, 1), :]

        def finish(sem):
            if an:
                part = rbuf.at[pl.ds(a0, an), pl.ds(0, NS - 1)]
                pltpu.make_async_copy(part, part, sem.at[idx]).wait()
            if bn:
                part = rbuf.at[pl.ds(b0, bn), pl.ds(0, NS)]
                pltpu.make_async_copy(part, part, sem.at[idx + 1]).wait()

        drains.append(lambda: finish(snd))
        return lambda: finish(rcv)

    drains = []

    stiff = cst[cid[0]]

    meta = [r[...].astype(F32) for r in (dst_r, src_r, tgt_r, kst_r)]

    def flat_row(m):
        return jnp.concatenate([m[0:1, :], m[1:2, :]], axis=1)

    dest = flat_row(meta[0])
    later = iota((128, 256), 1)
    rank = jnp.zeros((1, 256), F32)
    for h in range(2):
        column = jnp.broadcast_to(meta[0][h : h + 1, :], (128, 128)).T
        column = jnp.concatenate([column, column], axis=1)
        hit = (column == dest) & (iota((128, 256), 0) + 128.0 * h < later)
        rank = rank + jnp.sum(jnp.where(hit, 1.0, 0.0), axis=0, keepdims=True)
    slot = rank * 64.0 + dest
    source, target, kst = flat_row(meta[1]), flat_row(meta[2]), flat_row(meta[3])
    s_row = jnp.floor(source * (1.0 / 128.0))
    t_row = jnp.floor(target * (1.0 / 128.0))
    k_hi = kst.astype(BF16).astype(F32)
    k_mid = (kst - k_hi).astype(BF16).astype(F32)
    k_lo = kst - k_hi - k_mid
    rows = jnp.concatenate(
        [s_row, source - 128.0 * s_row, t_row, target - 128.0 * t_row, k_hi, k_mid, k_lo, jnp.ones((1, 256), F32)],
        axis=0,
    ).astype(BF16)
    onehot = jnp.where(iota((512, 256), 0) == slot, 1.0, 0.0).astype(BF16)
    packed = lax.dot_general(rows, onehot, NT, preferred_element_type=F32)
    valid = packed[7:8, :] > 0.5
    src_row = jnp.where(valid, packed[0:1, :], -1.0)
    picks = jnp.where(iota((128, 512), 0) == packed[1:2, :], 1.0, 0.0).astype(BF16)
    lsm[...] = jnp.concatenate([picks, picks], axis=0)
    rsm[...] = jnp.where(iota((64, 512), 0) == src_row, 1.0, 0.0)
    tgt = packed[2:3, :] * 128.0 + packed[3:4, :]
    kpk = packed[4:5, :] + packed[5:6, :] + packed[6:7, :]

    def edge_rows(ref, j, c):
        top = ref[j, c, pl.ds(15, 4, stride=16), :]
        bottom = ref[j, c, pl.ds(0, 4, stride=16), :]
        return jnp.where(ri == 0, top, bottom)

    def pack_radial(ref, out, spare):
        for j in range(4):
            tail = spare if (spare is not None and j == 0) else jnp.zeros((4, 128), F32)
            out[j] = jnp.concatenate([edge_rows(ref, j, c) for c in range(3)] + [tail], axis=0)

    def send_tangent(ref, dst):
        a = send(ref.at[:, :, pl.ds(48, 16), :], dst.at[0], nxt)
        b = send(ref.at[:, :, pl.ds(0, 16), :], dst.at[1], prv)
        return a, b

    def gather(ref, base):
        def column(j, carry):
            xs = jnp.concatenate([ref[j, c] for c in range(3)], axis=0)
            both = jnp.concatenate(split2(xs), axis=1)
            got = jnp.dot(both, lsm[...], preferred_element_type=F32)
            for c in range(3):
                picked = jnp.sum(got[c * 64 : (c + 1) * 64] * rsm[...], axis=0, keepdims=True)
                for sh in range(4):
                    wbuf[base + j * 4 + c, pl.ds(sh, 1), :] = picked[:, sh * 128 : (sh + 1) * 128]
            return carry

        for j in range(4):
            column(j, 0)

    def spare_rows(base, j, row):
        for sh in range(4):
            wbuf[base + j * 4 + 3, pl.ds(sh, 1), :] = row[:, sh * 128 : (sh + 1) * 128]

    def message(base):
        m = wbuf[pl.ds(base, 16)].reshape(64, 128)
        turned = jnp.concatenate([m, m], axis=0).T
        lane = lax.broadcasted_iota(jnp.int32, (64, 128), 1)
        return jnp.where(lane < 64, turned[0:64], turned[64:128])

    def unpack(m):
        both = jnp.concatenate([m, pltpu.roll(m, 64, 1)], axis=0).T
        return both[0:64].reshape(4, 16, 128)

    def fold_dots(ref, vref, half):
        lead = half * 4

        def block(c, acc):
            out = list(acc)
            for e in range(8):
                qv = [q[lead + i, c, 8 * e : 8 * e + 8, :] for i in range(4)]
                vv = [vref[j, c, 8 * e : 8 * e + 8, :] for j in range(4)]
                for j in range(4):
                    for i in range(4):
                        out[j * 4 + i] = out[j * 4 + i] + qv[i] * vv[j]
            return tuple(out)

        acc = lax.fori_loop(0, 3, block, tuple(jnp.zeros((8, 128), F32) for _ in range(16)))
        for j in range(4):
            for i in range(4):
                ref[pl.ds(j * 8 + lead + i, 1), :] = jnp.sum(acc[j * 4 + i], axis=0, keepdims=True)

    def gram(ref, scale, pairs):
        used = sorted({a for a, _ in pairs} | {e for _, e in pairs})

        def block(b, acc):
            c, r = b // 2, pl.multiple_of((b % 2) * 32, 32)
            out = list(acc)
            for h in range(4):
                qv = {i: q[i, c, pl.ds(r + 8 * h, 8), :] for i in used}
                sv = qv
                if scale is not None:
                    weight = ij[scale, c, pl.ds(r + 8 * h, 8), :]
                    sv = {i: qv[i] * weight for i in {a for a, _ in pairs}}
                for n, (a, e) in enumerate(pairs):
                    out[n] = out[n] + sv[a] * qv[e]
            return tuple(out)

        acc = lax.fori_loop(0, 6, block, tuple(jnp.zeros((8, 128), F32) for _ in pairs))
        for n, (a, e) in enumerate(pairs):
            row = jnp.sum(acc[n], axis=0, keepdims=True)
            ref[pl.ds(a * 8 + e, 1), :] = row
            if a != e:
                ref[pl.ds(e * 8 + a, 1), :] = row

    def upper(first, second):
        return [(a, e) for a in first for e in second if a <= e]

    def lane_totals(block):
        return jnp.sum(block.T, axis=0, keepdims=True)

    def spread(row):
        return jnp.broadcast_to(row * (1.0 / dofs), (128, 128)).T

    def put_rows(planes, e, row):
        planes[e] = jnp.broadcast_to(row, (NS, 128))

    def row_sum(rbuf, e):
        return jnp.sum(rbuf[e], axis=0, keepdims=True)

    def own_rows(rbuf, e):
        return rbuf[e, pl.ds(pl.multiple_of(ri * NS, NS), NS), :]

    loads[0].wait()
    gather(q, 16)
    rm[pl.ds(96, 32), :] = jnp.zeros((32, 128), F32)
    half = (range(0, 4), range(4, 8))
    gram(rm.at[pl.ds(32, 64)], None, upper(half[0], half[0]))
    loads[1].wait()
    gather(u, 0)
    fold_dots(rm, u, 0)
    loads[2].wait()
    got = jnp.dot(jnp.concatenate(split2(dg[...]), axis=1), lsm[...], preferred_element_type=F32)
    spare_rows(0, 0, jnp.sum(got * rsm[...], axis=0, keepdims=True))
    spare_rows(0, 1, tgt)
    spare_rows(0, 2, jnp.full((1, 512), stiff, F32))
    spare_rows(0, 3, kpk)
    for j in range(4):
        spare_rows(16, j, jnp.zeros((1, 512), F32))
    for e in range(2):
        pa[e] = message(16 * e)
    splat = jnp.full((8, 128), stiff, F32)
    dgs[0] = jnp.concatenate([dg[48:64, :], splat], axis=0)
    dgs[1] = jnp.concatenate([dg[0:16, :], splat], axis=0)
    dg_edge = jnp.where(ri == 0, dg[pl.ds(15, 4, stride=16), :], dg[pl.ds(0, 4, stride=16), :])
    pack_radial(u, rsnd.at[0], dg_edge)
    pack_radial(q, rsnd.at[1], None)

    pl.semaphore_wait(barrier, len(OFFSETS) + 1)
    swap_q = send(q.at[pl.ds(0, 4)], q.at[pl.ds(4, 4)], twin)
    touched = exchange(pa, ra, (0, 2), (0, 0))
    halo_q = send_tangent(q.at[pl.ds(0, 4)], qt.at[:, pl.ds(0, 4)])
    side_q = send(rsnd.at[1], qr.at[pl.ds(0, 4)], across)

    for j in range(4):
        for c in range(3):
            ij[j, c] = 1.0 / (stiff * 6.0 * kap[c, c] + dg[...] - shf[j])

    swap_q.wait_recv()
    fold_dots(rm, u, 1)
    gram(rm.at[pl.ds(32, 64)], None, upper(half[0], half[1]))
    gram(rm.at[pl.ds(32, 64)], None, upper(half[1], half[1]))
    put_rows(pa, 2, lane_totals(rm[pl.ds(0, 128), :]))
    summed = exchange(pa, ra, (2, 1), (2, 1))
    side_c = send(rsnd.at[0], ur, across)
    halo_d = (send(dgs.at[0], dgt.at[0], nxt), send(dgs.at[1], dgt.at[1], prv))
    halo_c = send_tangent(u, ut)

    def weighted(j, carry):
        part = rm.at[pl.ds(pl.multiple_of(128 + j * 64, 64), 64)]
        for a, e in ((0, 0), (0, 1), (1, 1)):
            gram(part, j, upper(half[a], half[e]))
        return carry

    lax.fori_loop(0, 4, weighted, 0)
    for e in range(2):
        put_rows(pb, 2 + e, lane_totals(rm[pl.ds(128 + e * 128, 128), :]))

    for c in halo_q + (side_q,):
        c.wait_recv()
    swap_t = send(qt.at[:, pl.ds(0, 4)], qt.at[:, pl.ds(4, 4)], twin)
    swap_r = send(qr.at[pl.ds(0, 4)], qr.at[pl.ds(4, 4)], twin)
    for c in halo_d + halo_c + (side_c,):
        c.wait_recv()
    for side in range(2):
        sv = jnp.concatenate([dgt[side, 16:24, :], dgt[side, 16:24, :]], axis=0)
        dv = dgt[side, 0:16, :]
        for j in range(4):
            for c in range(3):
                ijt[side, j, c] = 1.0 / (sv * 6.0 * kap[c, c] + dv - shf[j])
    dv = ur[0, 12:16, :]
    base = jnp.concatenate([stiff * 6.0 * kap[c, c] + dv for c in range(3)] + [jnp.full((4, 128), 2.0, F32)], axis=0)
    for j in range(4):
        ijr[j] = 1.0 / (base - shf[j])

    touched()
    us[...] = unpack(own_rows(ra, 0))
    qs[pl.ds(0, 4)] = unpack(own_rows(ra, 1))
    swap_s = send(qs.at[pl.ds(0, 4)], qs.at[pl.ds(4, 4)], twin)
    dv = us[0, 12:16, :]
    sv = us[2, 12:16, :]
    base = jnp.concatenate([sv * 6.0 * kap[c, c] + dv for c in range(3)] + [jnp.full((4, 128), 2.0, F32)], axis=0)
    for j in range(4):
        ijs[j] = 1.0 / (base - shf[j])
    kr = us[3, 12:16, :]
    for sh in range(4):
        tv = us[1, 12 + sh : 13 + sh, :]
        tr = jnp.floor(tv * (1.0 / 128.0))
        tl = tv - 128.0 * tr
        lanes = slice(sh * 128, (sh + 1) * 128)
        rtm[:, lanes] = jnp.where(iota((64, 128), 0) == tr, 1.0, 0.0).astype(BF16)
        krow[pl.ds(sh, 1), :] = kr[sh : sh + 1, :]
        lands = jnp.where(iota((128, 128), 0) == tl, 1.0, 0.0).astype(BF16)
        ltm[:, lanes] = lands
        ltm[:, 512 + sh * 128 : 640 + sh * 128] = lands

    summed()
    wide = spread(row_sum(ra, 2))
    acf[...] = wide[0:32].reshape(4, 8, 128)
    st_s[...] = wide[32:96].reshape(8, 8, 128)

    def mix(coef, j, qv):
        n = qv[0].shape[0]
        acc = None
        for i in range(8):
            term = jnp.broadcast_to(coef[j, pl.ds(i, 1), :], (n, 128)) * qv[i]
            acc = term if acc is None else acc + term
        return acc

    regions = (
        (12, lambda b: (b // 4, pl.multiple_of((b % 4) * 16, 16)),
         lambda r, j, a: r[j, a[0], pl.ds(a[1], 16), :], (u, q, ij, d)),
        (6, lambda b: (b // 3, b % 3),
         lambda r, j, a: r[a[0], j, a[1]], (ut, qt, ijt, dt)),
        (1, lambda b: b, lambda r, j, a: r[j], (us, qs, ijs, ds)),
        (1, lambda b: b, lambda r, j, a: r[j], (ur, qr, ijr, dr)),
    )

    def put(region, j, a, v):
        if region == 0:
            u[j, a[0], pl.ds(a[1], 16), :] = v
        elif region == 1:
            ut[a[0], j, a[1]] = v
        elif region == 2:
            us[j] = v
        else:
            ur[j] = v

    def first_update(which):
        for n in which:
            blocks, place, get, (ru, rq, _, _) = regions[n]

            def step(b, carry):
                a = place(b)
                qv = [get(rq, i, a) for i in range(8)]
                for j in range(4):
                    put(n, j, a, get(ru, j, a) - mix(acf, j, qv))
                return carry

            lax.fori_loop(0, blocks, step, 0)

    def update(rnd, which):
        for n in which:
            blocks, place, get, (ru, rq, rj, rd) = regions[n]

            def step(b, carry):
                a = place(b)
                qv = [get(rq, i, a) for i in range(8)]
                for j in range(4):
                    new = get(ru, j, a) + DAMPING * get(rd.at[rnd], j, a)
                    new = new + get(rj, j, a) * mix(cf.at[0], j, qv) - mix(cf.at[1], j, qv)
                    put(n, j, a, new)
                return carry

            lax.fori_loop(0, blocks, step, 0)

    for c in halo_c:
        c.wait_send()
        pending[:] = [t for t in pending if t is not c]
    first_update((0,))
    swap_t.wait_recv()
    swap_r.wait_recv()
    swap_s.wait_recv()
    first_update((1, 2, 3))

    row_in = lax.broadcasted_iota(jnp.int32, (16, 128), 0)
    lane_in = lax.broadcasted_iota(jnp.int32, (16, 128), 1)
    edge = row_in == 15 * (1 - ri)

    def apply(dref):
        def forces(j, carry):
            base = pl.multiple_of(j * 192, 192)
            for c in range(3):
                vs = us[j, c * 4 : c * 4 + 4, :] * krow[0:4, :]
                vh = vs.astype(BF16).astype(F32)
                for sh in range(4):
                    mask = rtm[:, sh * 128 : (sh + 1) * 128]
                    for e, part in enumerate((vh, vs - vh)):
                        full = jnp.broadcast_to(part[sh : sh + 1, :], (16, 128)).astype(BF16)
                        for t in range(4):
                            amat[pl.ds(base + c * 64 + 16 * t, 16), pl.ds(e * 512 + sh * 128, 128)] = (
                                mask[16 * t : 16 * t + 16] * full
                            )
            return carry

        lax.fori_loop(0, 4, forces, 0)
        land[...] = lax.dot_general(amat[...], ltm[...], NT, preferred_element_type=F32)

        def column(j, carry):
            for t in range(4):
                slab = slice(16 * t, 16 * t + 16)
                xs = [u[j, c, slab, :] for c in range(3)]
                base = dg[slab, :] - shf[j]
                for c in range(3):
                    v = xs[c]
                    before = ut[0, j, c] if t == 0 else u[j, c, 16 * t - 16 : 16 * t, :]
                    after = ut[1, j, c] if t == 3 else u[j, c, 16 * t + 16 : 16 * t + 32, :]
                    lap = 6.0 * v - before - after
                    lap = lap - jnp.where(row_in == 0, 0.0, pltpu.roll(v, 1, 0))
                    lap = lap - jnp.where(row_in == 15, 0.0, pltpu.roll(v, 15, 0))
                    beside = jnp.broadcast_to(ur[j, c * 4 + t : c * 4 + t + 1, :], (16, 128))
                    lap = lap - jnp.where(edge, beside, 0.0)
                    lap = lap - jnp.where(lane_in == 0, 0.0, pltpu.roll(v, 1, 1))
                    lap = lap - jnp.where(lane_in == 127, 0.0, pltpu.roll(v, 127, 1))
                    mixed = kap[c, c] * lap
                    for e in range(3):
                        if e != c:
                            mixed = mixed + kap[c, e] * xs[e]
                    out = stiff * mixed + base * v
                    out = out + land[pl.ds(pl.multiple_of(j * 192, 192) + c * 64 + 16 * t, 16), :]
                    w[j, c, slab, :] = out
                    dref[j, c, slab, :] = -(rho[j, c, slab, :] + out) * ij[j, c, slab, :]
            return carry

        lax.fori_loop(0, 4, column, 0)

    def coefficients(row, final):
        wide = spread(row)
        for j in range(4):
            b = wide[j * 8 : j * 8 + 8]
            e = wide[32 + j * 8 : 40 + j * 8]
            for i in range(8):
                e = e + mt_s[j, i] * b[i : i + 1, :]
            a = acf[j]
            if final:
                cf[0, j] = b
                cf[1, j] = a - DAMPING * e
            else:
                se = st_s[0] * e[0:1, :]
                for i in range(1, 8):
                    se = se + st_s[i] * e[i : i + 1, :]
                cf[0, j] = DAMPING * b
                cf[1, j] = DAMPING * (2.0 * e - se)
                acf[j] = a + DAMPING * (e - se)

    loads[3].wait()
    for rnd in range(3):
        last = rnd == 2
        dref = d.at[rnd]
        planes, rbuf = ((pb, rb), (pc, rc), (pd, rd))[rnd]
        apply(dref)
        for e in range(2):
            fold_dots(rm, w, e)
            fold_dots(rm.at[pl.ds(32, 32)], dref, e)
        put_rows(planes, 1, lane_totals(rm[pl.ds(0, 128), :]))
        nr = 3 if rnd == 0 else 1
        summed = exchange(planes, rbuf, (1, nr), (1, nr))
        if not last:
            gather(dref, 0)
            planes[0] = message(0)
            touched = exchange(planes, rbuf, (0, 1), (0, 0))
            pack_radial(dref, rsnd.at[2 + rnd], None)
            halo = send_tangent(dref, dt.at[rnd]) + (send(rsnd.at[2 + rnd], dr.at[rnd], across),)
        summed()
        if rnd == 0:
            for e in range(2):
                mt_s[pl.ds(2 * e, 2)] = spread(row_sum(rbuf, 2 + e)).reshape(2, 8, 8, 128)
        coefficients(row_sum(rbuf, 1), last)
        if not last:
            update(rnd, (0,))
            for c in halo:
                c.wait_recv()
            update(rnd, (1, 3))
            touched()
            ds[rnd] = unpack(own_rows(rbuf, 0))
            update(rnd, (2,))

    def finish(b, carry):
        c, r = b // 4, pl.multiple_of((b % 4) * 16, 16)
        here = (c, pl.ds(r, 16))
        qv = [q[i, c, pl.ds(r, 16), :] for i in range(8)]
        for j in range(4):
            res = mix(cf.at[0], j, qv) - rho[j, c, pl.ds(r, 16), :] - w[j, c, pl.ds(r, 16), :]
            new = u[j, c, pl.ds(r, 16), :] + DAMPING * res * ij[j, c, pl.ds(r, 16), :] + mix(cf.at[1], j, qv)
            or_h[j, c, pl.ds(r, 16), :] = res
            oc_h[j, c, pl.ds(r, 16), :] = new
        return carry

    lax.fori_loop(0, 12, finish, 0)
    for c in pending:
        c.wait_send()
    for wait in drains:
        wait()


def store(a, b, out_a, out_b, sem):
    copies = [pltpu.make_async_copy(a, out_a, sem.at[0]), pltpu.make_async_copy(b, out_b, sem.at[1])]
    for c in copies:
        c.start()
    for c in copies:
        c.wait()


def in_hbm(a):
    return pltpu.with_memory_space_constraint(a, pltpu.HBM)


def body(
    correction_guess, ritz_residual, ritz_basis, diagonal, coupling, class_ids,
    class_stiffness, shifts, contact_dest, contact_source, contact_target, contact_stiffness,
):
    cols, chans, tang, rloc, ax = correction_guess.shape
    devices = NX * NY * NZ * 2
    dofs = float(chans * tang * rloc * ax * devices)
    flat = (cols, chans, tang * rloc, ax)
    vm = pltpu.VMEM
    own = (4, 3, 64, 128)
    sheet = (4, 3, 16, 128)
    small = (4, 16, 128)
    scratch = [
        vm(own, F32), vm(own, F32), vm((8, 3, 64, 128), F32), vm((64, 128), F32), vm(own, F32), vm(own, F32),
        vm((3,) + own, F32),
        vm((2,) + sheet, F32), vm((2, 8, 3, 16, 128), F32), vm((2, 24, 128), F32), vm((2, 24, 128), F32),
        vm((2,) + sheet, F32), vm((2, 2) + sheet, F32),
        vm(small, F32), vm((8, 16, 128), F32), vm(small, F32), vm((2,) + small, F32),
        vm(small, F32), vm((8, 16, 128), F32), vm(small, F32), vm((2,) + small, F32), vm((4,) + small, F32),
        vm((256, 512), BF16), vm((64, 512), F32), vm((128, 1024), BF16), vm((64, 512), BF16), vm((32, 4, 128), F32),
        vm((768, 1024), BF16), vm((768, 128), F32), vm((8, 128), F32),
        vm((3, 64, 128), F32), vm((3, 128, 128), F32), vm((4, 64, 128), F32), vm((4, 128, 128), F32),
        vm((2, 64, 128), F32), vm((2, 128, 128), F32), vm((2, 64, 128), F32), vm((2, 128, 128), F32),
        vm((384, 128), F32),
        vm((2, 4, 8, 128), F32), vm((8, 8, 128), F32), vm((4, 8, 8, 128), F32), vm((4, 8, 128), F32),
        pltpu.SemaphoreType.DMA((4,)),
        pltpu.SemaphoreType.DMA((36,)), pltpu.SemaphoreType.DMA((36,)),
    ]
    anyspace = pl.BlockSpec(memory_space=pl.ANY)
    smem = pl.BlockSpec(memory_space=pltpu.SMEM)
    correction, residual = pl.pallas_call(
        functools.partial(kernel, dofs),
        out_shape=(jax.ShapeDtypeStruct(flat, F32), jax.ShapeDtypeStruct(flat, F32)),
        in_specs=[pl.BlockSpec(memory_space=pltpu.VMEM)] * 4 + [smem] * 4 + [anyspace] * 4,
        out_specs=(pl.BlockSpec(memory_space=pltpu.VMEM),) * 2,
        scratch_shapes=scratch,
        compiler_params=pltpu.CompilerParams(collective_id=0, has_side_effects=True, vmem_limit_bytes=16 * 1024 * 1024),
        name="sweeps",
    )(
        in_hbm(contact_dest.reshape(2, 128)), in_hbm(contact_source.reshape(2, 128)),
        in_hbm(contact_target.reshape(2, 128)), in_hbm(contact_stiffness.reshape(2, 128)),
        in_hbm(coupling), class_ids, in_hbm(class_stiffness), in_hbm(shifts),
        in_hbm(correction_guess.reshape(flat)), in_hbm(ritz_residual.reshape(flat)),
        in_hbm(ritz_basis.reshape(flat)), in_hbm(diagonal.reshape(tang * rloc, ax)),
    )
    correction, residual = pl.pallas_call(
        store,
        out_shape=(jax.ShapeDtypeStruct(flat, F32), jax.ShapeDtypeStruct(flat, F32)),
        in_specs=[anyspace] * 2,
        out_specs=(anyspace, anyspace),
        scratch_shapes=[pltpu.SemaphoreType.DMA((2,))],
        compiler_params=pltpu.CompilerParams(vmem_limit_bytes=1024 * 1024),
        name="store",
    )(correction, residual)
    shape = correction_guess.shape
    return correction.reshape(shape), residual.reshape(shape)


def solution(mesh):
    split = Mesh(
        mesh.devices.reshape(NX, NY, NZ, mesh.shape["radial"], mesh.shape["col"]),
        ("sector_0", "sector_1", "sector_2", "radial", "col"),
    )
    field = P("col", None, SECTOR, "radial", None)
    placed = (
        field, field, field, P(SECTOR, "radial", None), P(), P(SECTOR), P(), P("col"),
        P(SECTOR_RADIAL, None), P(SECTOR_RADIAL), P(SECTOR_RADIAL), P(SECTOR_RADIAL),
    )
    return jax.shard_map(body, mesh=split, in_specs=placed, out_specs=(field, field), check_vma=False)
```
